32 devices in a mesh: shard: 4 (over z), context: 4 (over x, core), tensor: 2 (over y).
Axes of the slice: x: 2, y: 2, z: 4, core: 2. Of those that a mesh axis runs over, the one named last changes fastest.
Arguments:
- tokens: bfloat16 [8, 1024, 1408], P('shard', 'context'), may hold values from -6 to 6
- skip_in: bfloat16 [8, 1024, 1408], P('shard', 'context'), may hold values from -6 to 6
- text_in: bfloat16 [8, 333, 1408], P('shard'), may hold values from -6 to 6
- grid_pos: int32 [8, 1024, 2], P('shard', 'context'), may hold values from 0 to 63
- time_ids: int32 [8], P('shard'), may hold values from 0 to 999
- cotangent: bfloat16 [8, 1024, 1408], P('shard', 'context'), may hold values from -6 to 6
- skip_weight: bfloat16 [2, 1408, 1408], P(None, ('shard', 'tensor')), may hold values from -0.109375 to 0.109375
- shift_weight: bfloat16 [1408, 1408], P(('shard', 'tensor')), may hold values from -0.15625 to 0.15625
- triple_weight: bfloat16 [1408, 3, 1408], P('shard', None, 'tensor'), may hold values from -0.15625 to 0.15625
- self_out_weight: bfloat16 [1408, 1408], P('tensor', 'shard'), may hold values from -0.4375 to 0.4375
- cross_q_weight: bfloat16 [1408, 1408], P('shard', 'tensor'), may hold values from -0.15625 to 0.15625
- cross_kv_weight: bfloat16 [1408, 2, 1408], P('shard', None, 'tensor'), may hold values from -0.15625 to 0.15625
- cross_out_weight: bfloat16 [1408, 1408], P('tensor', 'shard'), may hold values from -0.3125 to 0.3125
- up_weight: bfloat16 [1408, 6144], P('shard', 'tensor'), may hold values from -0.15625 to 0.15625
- down_weight: bfloat16 [6144, 1408], P('tensor', 'shard'), may hold values from -0.078125 to 0.078125
- norm_gains: float32 [4, 1408], replicated, may hold values from 0.25 to 1.75
- norm_biases: float32 [4, 1408], replicated, may hold values from -1.5 to 1.5
- head_gains: float32 [4, 88], replicated, may hold values from 0.25 to 1.75
- head_biases: float32 [4, 88], replicated, may hold values from -1.5 to 1.5
- width_biases: float32 [5, 1408], replicated, may hold values from -1.5 to 1.5
- column_biases: float32 [6, 1408], replicated, may hold values from -1.5 to 1.5
- hidden_biases: float32 [6144], replicated, may hold values from -1.5 to 1.5
Outputs:
- output: float32 [8, 1024, 1408], P('shard', 'context')
- grad_tokens: float32 [8, 1024, 1408], P('shard', 'context')
- grad_skip: float32 [8, 1024, 1408], P('shard', 'context')
- grad_text: float32 [8, 333, 1408], P('shard', None, ('context', 'tensor'))
- grad_skip_weight: float32 [2, 1408, 1408], P(None, ('shard', 'tensor'))
- grad_shift_weight: float32 [1408, 1408], P(('shard', 'tensor'))
- grad_triple_weight: float32 [1408, 3, 1408], P('shard', None, 'tensor')
- grad_self_out_weight: float32 [1408, 1408], P('tensor', 'shard')
- grad_cross_q_weight: float32 [1408, 1408], P('shard', 'tensor')
- grad_cross_kv_weight: float32 [1408, 2, 1408], P('shard', None, 'tensor')
- grad_cross_out_weight: float32 [1408, 1408], P('tensor', 'shard')
- grad_up_weight: float32 [1408, 6144], P('shard', 'tensor')
- grad_down_weight: float32 [6144, 1408], P('tensor', 'shard')
- grad_norm_gains: float32 [4, 1408], replicated
- grad_norm_biases: float32 [4, 1408], replicated
- grad_head_gains: float32 [4, 88], replicated
- grad_head_biases: float32 [4, 88], replicated
- grad_width_biases: float32 [5, 1408], replicated
- grad_column_biases: float32 [6, 1408], replicated
- grad_hidden_biases: float32 [6144], replicated
The draws below stay inside these ranges and needn't reach their ends.
All inputs are finite; a program needn't handle non-finite values.
Results may differ from the reference program's by a relative error of at most 0.02.
Values may be sent and summed in bfloat16 or wider, within the bound.
A program may use at most 320 MiB of HBM per device.

```python
import math
import jax
import jax.numpy as jnp
from jax import lax

D = 1408
HEADS = 16
HD = 88
FF = 6144
TXT = 333
LENGTH = 1024
BATCH = 8


def set_ends(values, rng, low, top_value):
    place = [jax.random.randint(jax.random.fold_in(rng, axis), (), 0, length) for axis, length in enumerate(values.shape)]
    main_axis = values.shape.index(max(values.shape))
    next_to = place[:main_axis] + [(place[main_axis] + 1) % values.shape[main_axis]] + place[main_axis + 1:]
    return values.at[tuple(place)].set(low).at[tuple(next_to)].set(top_value)


def shard_levels(own_key, shape, split, smallest, largest):
    def one(position, blocks):
        steps = jax.random.uniform(jax.random.fold_in(jax.random.fold_in(own_key, 6), position), (blocks,), jnp.float32, smallest / len(split), largest / len(split))
        return jnp.repeat(jnp.exp(steps), shape[position] // blocks).reshape((-1,) + (1,) * (len(shape) - position - 1))

    loudness = one(*split[0])
    for cut in split[1:]:
        loudness = loudness * one(*cut)
    return loudness


def gaussian(rng, dims, width, most, shards=(), held_as=jnp.bfloat16):
    values = jax.random.normal(rng, dims, jnp.float32) * width
    if len(shards) > 0:
        values = shard_levels(rng, dims, shards, -0.22, 0.18) * values
    return jnp.clip(values, min=-most, max=most).astype(held_as)


def setup_inputs(seed: int = 0) -> dict:
    splits = jax.random.split(jax.random.key(seed), 23)
    tokens = gaussian(splits[0], (BATCH, LENGTH, D), 1.0, 6.0, ((0, 4), (1, 4)))
    skip_in = gaussian(splits[1], (BATCH, LENGTH, D), 1.0, 6.0, ((0, 4), (1, 4)))
    text_in = gaussian(splits[2], (BATCH, TXT, D), 1.0, 6.0, ((0, 4),))
    grid_pos = set_ends(jax.random.randint(splits[3], (BATCH, LENGTH, 2), 0, 64), jax.random.fold_in(splits[3], 1), 0, 63).astype(jnp.int32)
    time_ids = set_ends(jax.random.randint(splits[4], (BATCH,), 0, 1000), jax.random.fold_in(splits[4], 1), 0, 999).astype(jnp.int32)
    cotangent = gaussian(splits[5], (BATCH, LENGTH, D), 1.0, 6.0, ((0, 4), (1, 4)))
    skip_weight = gaussian(splits[6], (2, D, D), (2 * D) ** -0.5, 0.109375, ((1, 8),))
    shift_weight = gaussian(splits[7], (D, D), D ** -0.5, 0.15625, ((0, 8),))
    triple_weight = gaussian(splits[8], (D, 3, D), D ** -0.5, 0.15625, ((0, 4), (2, 2)))
    self_out_weight = gaussian(splits[9], (D, D), (D // 8) ** -0.5, 0.4375, ((0, 2), (1, 4)))
    cross_q_weight = gaussian(splits[10], (D, D), D ** -0.5, 0.15625, ((0, 4), (1, 2)))
    cross_kv_weight = gaussian(splits[11], (D, 2, D), D ** -0.5, 0.15625, ((0, 4), (2, 2)))
    cross_out_weight = gaussian(splits[12], (D, D), (D // 4) ** -0.5, 0.3125, ((0, 2), (1, 4)))
    up_weight = gaussian(splits[13], (D, FF), D ** -0.5, 0.15625, ((0, 4), (1, 2)))
    down_weight = gaussian(splits[14], (FF, D), FF ** -0.5, 0.078125, ((0, 2), (1, 4)))
    norm_gains = jnp.clip(1.0 + 0.15 * jax.random.normal(splits[15], (4, D), jnp.float32), 0.25, 1.75)
    norm_biases = gaussian(splits[16], (4, D), 0.3, 1.5, (), jnp.float32)
    head_gains = jnp.clip(1.0 + 0.15 * jax.random.normal(splits[17], (4, HD), jnp.float32), 0.25, 1.75)
    head_biases = gaussian(splits[18], (4, HD), 0.3, 1.5, (), jnp.float32)
    width_biases = gaussian(splits[19], (5, D), 0.3, 1.5, (), jnp.float32)
    column_biases = gaussian(splits[20], (6, D), 0.3, 1.5, (), jnp.float32)
    hidden_biases = gaussian(splits[21], (FF,), 0.3, 1.5, (), jnp.float32)
    return {"tokens": tokens, "skip_in": skip_in, "text_in": text_in, "grid_pos": grid_pos, "time_ids": time_ids, "cotangent": cotangent, "skip_weight": skip_weight, "shift_weight": shift_weight, "triple_weight": triple_weight, "self_out_weight": self_out_weight, "cross_q_weight": cross_q_weight, "cross_kv_weight": cross_kv_weight, "cross_out_weight": cross_out_weight, "up_weight": up_weight, "down_weight": down_weight, "norm_gains": norm_gains, "norm_biases": norm_biases, "head_gains": head_gains, "head_biases": head_biases, "width_biases": width_biases, "column_biases": column_biases, "hidden_biases": hidden_biases}


@jax.custom_vjp
def low(v):
    return lax.optimization_barrier(v.astype(jnp.bfloat16)).astype(jnp.float32)

@jax.custom_vjp
def low_back(v):
    return v

def low_keep(v):
    return (low(v), None)

def low_pass(kept, grad):
    return (grad,)

def back_keep(v):
    return (v, None)

def back_low(kept, grad):
    return (low(grad),)
low.defvjp(low_keep, low_pass)
low_back.defvjp(back_keep, back_low)
epsilon = 1e-06
highest = lax.Precision.HIGHEST

def product(left_side, right_side):
    return jnp.dot(left_side, right_side, precision=highest)

def layer_norm(values, scale_vec, offset):
    center = values - lax.optimization_barrier(jnp.mean(values, -1, keepdims=True))
    spread = lax.optimization_barrier(jnp.mean(center * center, -1, keepdims=True))
    return center * lax.rsqrt(spread + epsilon) * scale_vec + offset

def rotary_tables(grid_rows, head_size):
    quarter = head_size // 4
    frequencies = 1.0 / 10000.0 ** (jnp.arange(quarter, dtype=jnp.float32) * 2.0 / (head_size // 2))
    row_angle = grid_rows[:, 0:1].astype(jnp.float32) * frequencies
    col_angle = grid_rows[:, 1:2].astype(jnp.float32) * frequencies
    angles = jnp.concatenate([row_angle, row_angle, col_angle, col_angle], 1)
    return (jnp.cos(angles)[:, None, :], jnp.sin(angles)[:, None, :])

def rotate(values, cosine, sine_rows):
    quarter = values.shape[-1] // 4
    part_one = values[..., :quarter]
    part_two = values[..., quarter:2 * quarter]
    part_three = values[..., 2 * quarter:3 * quarter]
    part_four = values[..., 3 * quarter:]
    turned = jnp.concatenate([-part_two, part_one, -part_four, part_three], -1)
    return values * cosine + turned * sine_rows

def time_vector(time_stamp, model_width):
    half_width = model_width // 2
    frequencies = jnp.exp(-math.log(10000.0) * jnp.arange(half_width, dtype=jnp.float32) / half_width)
    angles = time_stamp.astype(jnp.float32) * frequencies
    return jnp.concatenate([jnp.cos(angles), jnp.sin(angles)])

def attend(queries, key_rows, value_rows):
    score_scale = queries.shape[-1] ** (-0.5)
    total_rows = queries.shape[0]
    block_rows = min(512, total_rows)
    block_count = total_rows // block_rows

    def one_block(row_block):
        scores = low_back(jnp.einsum('qhd,khd->hqk', row_block, key_rows, precision=highest) * score_scale)
        exponent = jnp.exp(scores - lax.optimization_barrier(jnp.max(scores, -1, keepdims=True)))
        weights_full = exponent / lax.optimization_barrier(jnp.sum(exponent, -1, keepdims=True))
        return jnp.einsum('hqk,khd->qhd', low(weights_full), value_rows, precision=highest)
    stacked = queries.reshape(block_count, block_rows, queries.shape[1], queries.shape[2])
    return lax.map(jax.checkpoint(one_block), stacked).reshape(queries.shape)

def forward(tokens_f, skip_f, text_f, cosine, sine_rows, time_silu, params):
    skip_weight, shift_weight, triple_weight, self_out_weight, cross_q_weight, cross_kv_weight, cross_out_weight, up_weight, down_weight, norm_gains, norm_biases, head_gains, head_biases, width_biases, column_biases, hidden_biases = params
    seq_len = tokens_f.shape[0]
    model_width = tokens_f.shape[1]
    text_len = text_f.shape[0]
    head_shape = (seq_len, HEADS, HD)
    text_shape = (text_len, HEADS, HD)
    summed = low_back(product(tokens_f, skip_weight[0]) + product(skip_f, skip_weight[1]) + width_biases[0])
    resid_zero = layer_norm(summed, norm_gains[0], norm_biases[0])
    shift_row = product(low(time_silu)[None, :], shift_weight)[0] + width_biases[1]
    normed_one = low(layer_norm(resid_zero, norm_gains[1], norm_biases[1]) + shift_row)
    triple = low_back(jnp.einsum('td,dcn->tcn', normed_one, triple_weight, precision=highest) + column_biases[0:3])
    queries = low_back(low(rotate(layer_norm(triple[:, 0].reshape(head_shape), head_gains[0], head_biases[0]), cosine, sine_rows)))
    key_rows = low_back(low(rotate(layer_norm(triple[:, 1].reshape(head_shape), head_gains[1], head_biases[1]), cosine, sine_rows)))
    value_rows = low_back(low(triple[:, 2].reshape(head_shape)))
    self_mix = low_back(low(attend(queries, key_rows, value_rows).reshape(seq_len, model_width)))
    resid_one = resid_zero + low_back(product(self_mix, self_out_weight) + width_biases[2])
    normed_two = low(layer_norm(resid_one, norm_gains[2], norm_biases[2]))
    cross_raw = low_back(product(normed_two, cross_q_weight) + column_biases[3]).reshape(head_shape)
    cross_query = low(rotate(layer_norm(cross_raw, head_gains[2], head_biases[2]), cosine, sine_rows))
    pair = low_back(jnp.einsum('td,dcn->tcn', text_f, cross_kv_weight, precision=highest) + column_biases[4:6])
    cross_key = low(layer_norm(pair[:, 0].reshape(text_shape), head_gains[3], head_biases[3]))
    cross_value = low(pair[:, 1].reshape(text_shape))
    cross_mix = low_back(low(attend(cross_query, cross_key, cross_value).reshape(seq_len, model_width)))
    resid_two = resid_one + low_back(product(cross_mix, cross_out_weight) + width_biases[3])
    normed_three = low(layer_norm(resid_two, norm_gains[3], norm_biases[3]))
    hidden = low_back(product(normed_three, up_weight) + hidden_biases)
    active = low(jax.nn.gelu(hidden, approximate=True))
    return resid_two + low_back(product(active, down_weight) + width_biases[4])

def reference(tokens, skip_in, text_in, grid_pos, time_ids, cotangent, skip_weight, shift_weight, triple_weight, self_out_weight, cross_q_weight, cross_kv_weight, cross_out_weight, up_weight, down_weight, norm_gains, norm_biases, head_gains, head_biases, width_biases, column_biases, hidden_biases):
    params = (skip_weight.astype(jnp.float32), shift_weight.astype(jnp.float32), triple_weight.astype(jnp.float32), self_out_weight.astype(jnp.float32), cross_q_weight.astype(jnp.float32), cross_kv_weight.astype(jnp.float32), cross_out_weight.astype(jnp.float32), up_weight.astype(jnp.float32), down_weight.astype(jnp.float32), norm_gains, norm_biases, head_gains, head_biases, width_biases, column_biases, hidden_biases)
    zero_grads = jax.tree.map(jnp.zeros_like, params)

    def per_sequence(totals, inputs_now):
        tok_rows, skip_rows, text_rows, grid_rows, time_stamp, cot_rows = inputs_now
        cosine, sine_rows = rotary_tables(grid_rows, HD)
        time_silu = jax.nn.silu(time_vector(time_stamp, D))

        def closed(tokens_f, skip_f, text_f, param_list):
            return forward(tokens_f, skip_f, text_f, cosine, sine_rows, time_silu, param_list)
        result, pullback = jax.vjp(closed, tok_rows.astype(jnp.float32), skip_rows.astype(jnp.float32), text_rows.astype(jnp.float32), params)
        grad_tok, grad_skp, grad_txt, grad_params = pullback(cot_rows.astype(jnp.float32))
        return (jax.tree.map(jnp.add, totals, grad_params), (result, grad_tok, grad_skp, grad_txt))
    totals, stacked = lax.scan(per_sequence, zero_grads, (tokens, skip_in, text_in, grid_pos, time_ids, cotangent))
    return (stacked[0], stacked[1], stacked[2], stacked[3], totals[0], totals[1], totals[2], totals[3], totals[4], totals[5], totals[6], totals[7], totals[8], totals[9], totals[10], totals[11], totals[12], totals[13], totals[14], totals[15])
```

```python
import math

import jax
import jax.numpy as jnp
from jax import lax
from jax.sharding import PartitionSpec as P

epsilon = 1e-06
BF = jnp.bfloat16
F32 = jnp.float32


def matmul(left_side, right_side):
    return jnp.dot(left_side, right_side, preferred_element_type=F32)


def contract(form, left_side, right_side):
    return jnp.einsum(form, left_side, right_side, preferred_element_type=F32)


def contract_rows(left_side, right_side):
    return lax.dot_general(left_side, right_side, (((0,), (0,)), ((), ())), preferred_element_type=F32)


def contract_cols(left_side, right_side):
    return lax.dot_general(left_side, right_side, (((1,), (1,)), ((), ())), preferred_element_type=F32)


def layer_norm(values, scale_vec, offset):
    center = values - jnp.mean(values, -1, keepdims=True)
    spread = jnp.mean(center * center, -1, keepdims=True)
    return center * lax.rsqrt(spread + epsilon) * scale_vec + offset


def rotary_tables(grid_rows, head_size):
    quarter = head_size // 4
    frequencies = 1.0 / 10000.0 ** (jnp.arange(quarter, dtype=F32) * 2.0 / (head_size // 2))
    row_angle = grid_rows[:, 0:1].astype(F32) * frequencies
    col_angle = grid_rows[:, 1:2].astype(F32) * frequencies
    angles = jnp.concatenate([row_angle, row_angle, col_angle, col_angle], 1)
    return (jnp.cos(angles)[:, None, :], jnp.sin(angles)[:, None, :])


def rotate(values, cosine, sine_rows):
    quarter = values.shape[-1] // 4
    one = values[..., :quarter]
    two = values[..., quarter : 2 * quarter]
    three = values[..., 2 * quarter : 3 * quarter]
    four = values[..., 3 * quarter :]
    turned = jnp.concatenate([-two, one, -four, three], -1)
    return values * cosine + turned * sine_rows


def time_silu(stamps, model_width):
    half_width = model_width // 2
    frequencies = jnp.exp(-math.log(10000.0) * jnp.arange(half_width, dtype=F32) / half_width)
    angles = stamps.astype(F32)[:, None] * frequencies
    return jax.nn.silu(jnp.concatenate([jnp.cos(angles), jnp.sin(angles)], 1)).astype(BF)


def attention_forward(queries, key_rows, value_rows):
    score_scale = queries.shape[-1] ** (-0.5)
    scores = contract("qhd,khd->hqk", queries, key_rows) * score_scale
    row_max = jnp.max(scores, -1, keepdims=True)
    exponent = jnp.exp(scores - row_max)
    weight_sum = jnp.sum(exponent, -1, keepdims=True)
    weights_low = (exponent / weight_sum).astype(BF)
    mixture = contract("hqk,khd->qhd", weights_low, value_rows)
    return (mixture.astype(BF), (row_max + jnp.log(weight_sum))[..., 0])


def attention_backward(queries, key_rows, value_rows, log_sums, grad_mix):
    score_scale = queries.shape[-1] ** (-0.5)
    scores = contract("qhd,khd->hqk", queries, key_rows) * score_scale
    weights_full = jnp.exp(scores - log_sums[..., None])
    grad_weights = contract("qhd,khd->hqk", grad_mix, value_rows)
    inner = jnp.sum(weights_full * grad_weights, -1, keepdims=True)
    grad_scores = (weights_full * (grad_weights - inner)).astype(BF)
    query_grad = contract("hqk,khd->qhd", grad_scores, key_rows) * score_scale
    key_grad = contract("hqk,qhd->khd", grad_scores, queries) * score_scale
    value_grad = contract("hqk,qhd->khd", weights_full.astype(BF), grad_mix)
    return (query_grad, key_grad, value_grad)


def on_device(
    tokens, skip_in, text_in, grid_pos, time_ids, cotangent,
    skip_weight, shift_weight, triple_weight, self_out_weight, cross_q_weight,
    cross_kv_weight, cross_out_weight, up_weight, down_weight,
    norm_gains, norm_biases, head_gains, head_biases, width_biases, column_biases, hidden_biases,
):
    batch, local_len, width = tokens.shape
    text_len = text_in.shape[1]
    head_size = head_gains.shape[1]
    z = lax.axis_index("shard")
    k = lax.axis_index("context")
    y = lax.axis_index("tensor")
    nz, nk, ny = lax.axis_size("shard"), lax.axis_size("context"), lax.axis_size("tensor")
    assert batch == ny == 2
    rows_z = triple_weight.shape[0]
    half_cols = triple_weight.shape[2]
    half_hidden = up_weight.shape[1]
    cb = half_cols // nk
    hb = half_hidden // nk
    eb = width // nk
    hh = cb // head_size
    heads = ny * hh
    length = local_len * nk
    sequences = batch * nz
    swap = [(0, 1), (1, 0)]

    def mine(values):
        return lax.dynamic_index_in_dim(values, y, 0, keepdims=False)

    def block(values, size, axis):
        return lax.dynamic_slice_in_dim(values, k * size, size, axis)

    def other(values):
        return lax.ppermute(values, "tensor", swap)

    def pair(values):
        return (values, other(values))

    def gather_rows(values):
        return lax.all_gather(values, "context", axis=0, tiled=True)

    def scatter_rows(values):
        return lax.psum_scatter(values.astype(BF), "context", scatter_dimension=0, tiled=True).astype(F32)

    def by_batch(own, theirs):
        first = jnp.where(y == 0, own, theirs)
        second = jnp.where(y == 0, theirs, own)
        return jnp.stack([first, second])

    def gather_first(values):
        return pair(lax.all_gather(values, "shard", axis=0, tiled=True))

    def gather_last(values):
        got = lax.all_gather(values, "shard", axis=0, tiled=False)
        return pair(jnp.transpose(got, (1, 0, 2)).reshape(values.shape[0], -1))

    skip_block = lax.all_gather(block(skip_weight, eb, 2), ("shard", "tensor"), axis=1, tiled=True).reshape(2 * width, eb)
    triple_full = gather_first(block(triple_weight, cb, 2).reshape(rows_z, 3 * cb))
    self_out_full = gather_last(block(self_out_weight, cb, 0))
    cross_q_full = gather_first(block(cross_q_weight, cb, 1))
    cross_kv_full = gather_first(block(cross_kv_weight, cb, 2).reshape(rows_z, 2 * cb))
    cross_out_full = gather_last(block(cross_out_weight, cb, 0))
    up_full = gather_first(block(up_weight, hb, 1))
    down_full = gather_last(block(down_weight, hb, 0))

    def own_columns(values, size, half):
        last = values.ndim - 1
        first = lax.dynamic_slice_in_dim(values, y * half + k * size, size, last)
        second = lax.dynamic_slice_in_dim(values, (1 - y) * half + k * size, size, last)
        return (first, second)

    tok_rows, skip_rows, cot_rows = mine(tokens), mine(skip_in), mine(cotangent)
    text_rows = mine(text_in)
    grid_all = gather_rows(mine(grid_pos))
    cosine, sine_rows = rotary_tables(grid_all, head_size)
    times = lax.all_gather(time_ids, "shard", axis=0, tiled=True)
    silu_all = time_silu(times, width)
    shift_rows_count = shift_weight.shape[0]
    silu_rows = lax.dynamic_slice_in_dim(silu_all, (z * ny + y) * shift_rows_count, shift_rows_count, 1)
    shift_row = lax.psum_scatter(matmul(silu_rows, shift_weight), ("shard", "tensor"), scatter_dimension=0, tiled=True)[0]
    shift_row = shift_row + width_biases[1]

    tok_all = gather_rows(jnp.concatenate([tok_rows, skip_rows], 1))
    summed_block = matmul(tok_all, skip_block)
    summed = lax.all_to_all(summed_block, "context", split_axis=0, concat_axis=1, tiled=True) + width_biases[0]

    def first_piece(summed_in, shift_in, gain_rows, bias_rows):
        resid_out = layer_norm(summed_in, gain_rows[0], bias_rows[0])
        return (resid_out, layer_norm(resid_out, gain_rows[1], bias_rows[1]) + shift_in)

    (resid_zero, normed_one), pull_first = jax.vjp(first_piece, summed, shift_row, norm_gains, norm_biases)
    normed_one_all = gather_rows(normed_one.astype(BF))
    triple_bias = own_columns(column_biases[0:3], cb, half_cols)

    def to_heads(parts, count):
        return jnp.concatenate([p.reshape(p.shape[0], count, hh, head_size) for p in parts], 2)

    def from_heads(values):
        rows, count = values.shape[0], values.shape[1]
        return (values[:, :, :hh].reshape(rows, count * cb), values[:, :, hh:].reshape(rows, count * cb))

    triple = to_heads([matmul(normed_one_all, w) + b.reshape(1, -1) for w, b in zip(triple_full, triple_bias)], 3)

    def self_piece(triple_in, gain_rows, bias_rows):
        queries = rotate(layer_norm(triple_in[:, 0], gain_rows[0], bias_rows[0]), cosine, sine_rows)
        key_rows = rotate(layer_norm(triple_in[:, 1], gain_rows[1], bias_rows[1]), cosine, sine_rows)
        return (queries, key_rows, triple_in[:, 2])

    (query, key, value), pull_self = jax.vjp(self_piece, triple, head_gains, head_biases)
    query, key, value = query.astype(BF), key.astype(BF), value.astype(BF)
    mix, self_sums = attention_forward(query, key, value)
    mix_parts = from_heads(mix[:, None])
    resid_one = resid_zero + (
        scatter_rows(matmul(mix_parts[0], self_out_full[0]) + matmul(mix_parts[1], self_out_full[1])) + width_biases[2]
    )

    def second_piece(resid_in, gain_rows, bias_rows):
        return layer_norm(resid_in, gain_rows[2], bias_rows[2])

    normed_two, pull_second = jax.vjp(second_piece, resid_one, norm_gains, norm_biases)
    normed_two_all = gather_rows(normed_two.astype(BF))
    cq_bias = own_columns(column_biases[3], cb, half_cols)
    kv_bias = own_columns(column_biases[4:6], cb, half_cols)
    cross_raw = to_heads([matmul(normed_two_all, w) + b.reshape(1, -1) for w, b in zip(cross_q_full, cq_bias)], 1)
    pair_raw = to_heads([matmul(text_rows, w) + b.reshape(1, -1) for w, b in zip(cross_kv_full, kv_bias)], 2)

    def cross_piece(query_in, pair_in, gain_rows, bias_rows):
        queries = rotate(layer_norm(query_in[:, 0], gain_rows[2], bias_rows[2]), cosine, sine_rows)
        key_rows = layer_norm(pair_in[:, 0], gain_rows[3], bias_rows[3])
        return (queries, key_rows, pair_in[:, 1])

    (cq, ck, cv), pull_cross = jax.vjp(cross_piece, cross_raw, pair_raw, head_gains, head_biases)
    cq, ck, cv = cq.astype(BF), ck.astype(BF), cv.astype(BF)
    cross_mix, cross_sums = attention_forward(cq, ck, cv)
    cross_parts = from_heads(cross_mix[:, None])
    resid_two = resid_one + (
        scatter_rows(matmul(cross_parts[0], cross_out_full[0]) + matmul(cross_parts[1], cross_out_full[1])) + width_biases[3]
    )

    def third_piece(resid_in, gain_rows, bias_rows):
        return layer_norm(resid_in, gain_rows[3], bias_rows[3])

    normed_three, pull_third = jax.vjp(third_piece, resid_two, norm_gains, norm_biases)
    normed_three_all = gather_rows(normed_three.astype(BF))
    hidden_bias = own_columns(hidden_biases, hb, half_hidden)

    def gelu_piece(hidden_in):
        return jax.nn.gelu(hidden_in, approximate=True)

    active, pull_gelu = [], []
    for w, b in zip(up_full, hidden_bias):
        act, pull = jax.vjp(gelu_piece, matmul(normed_three_all, w) + b)
        active.append(act.astype(BF))
        pull_gelu.append(pull)
    result = resid_two + (
        scatter_rows(matmul(active[0], down_full[0]) + matmul(active[1], down_full[1])) + width_biases[4]
    )
    result_low = result.astype(BF)
    result_out = by_batch(result_low, other(result_low)).astype(F32)

    def reduce_first(parts, scale_rows=None):
        total = parts[0] + other(parts[1].astype(BF)).astype(F32)
        return lax.psum_scatter(total.astype(BF), "shard", scatter_dimension=0, tiled=True)

    def reduce_last(parts):
        total = parts[0] + other(parts[1].astype(BF)).astype(F32)
        rows = total.shape[0]
        total = jnp.transpose(total.astype(BF).reshape(rows, nz, rows_z), (1, 0, 2))
        return lax.psum_scatter(total, "shard", scatter_dimension=0, tiled=True)[0]

    def spread(values):
        return lax.all_gather(values, "context", axis=0, tiled=False)

    def spread_last(values, count):
        got = spread(values).reshape(nk, values.shape[0], count, -1)
        got = jnp.transpose(got, (1, 2, 0, 3)).reshape(values.shape[0], count, -1)
        return got.astype(F32)

    cot_all = gather_rows(cot_rows)
    grad_out = cot_rows.astype(F32)
    down_grad = reduce_last([contract_rows(a, cot_all) for a in active])
    hidden_grad = [pull(contract_cols(cot_all, w))[0].astype(BF) for pull, w in zip(pull_gelu, down_full)]
    up_grad = reduce_first([contract_rows(normed_three_all, h) for h in hidden_grad])
    third_grads = pull_third(
        scatter_rows(contract_cols(hidden_grad[0], up_full[0]) + contract_cols(hidden_grad[1], up_full[1]))
    )
    resid_two_grad = grad_out + third_grads[0]
    grad_two_low = resid_two_grad.astype(BF)
    grad_two_all = gather_rows(grad_two_low)
    cross_out_grad = reduce_last([contract_rows(p, grad_two_all) for p in cross_parts])
    cross_mix_grad = to_heads([contract_cols(grad_two_all, w).astype(BF) for w in cross_out_full], 1)[:, 0]
    cq_back, ck_back, cv_back = attention_backward(cq, ck, cv, cross_sums, cross_mix_grad)
    cross_grads = pull_cross((cq_back, ck_back, cv_back))
    cross_grad_low = from_heads(cross_grads[0].astype(BF))
    pair_low = from_heads(cross_grads[1].astype(BF))
    cross_q_grad = reduce_first([contract_rows(normed_two_all, g) for g in cross_grad_low])
    cross_kv_grad = reduce_first([contract_rows(text_rows, g) for g in pair_low])
    text_part = contract_cols(pair_low[0], cross_kv_full[0]) + contract_cols(pair_low[1], cross_kv_full[1])
    text_part = lax.psum_scatter(text_part.astype(BF), "context", scatter_dimension=1, tiled=True)
    text_cols = text_part.shape[1] // ny
    text_mine = lax.dynamic_slice_in_dim(text_part, y * text_cols, text_cols, 1)
    text_theirs = other(lax.dynamic_slice_in_dim(text_part, (1 - y) * text_cols, text_cols, 1))
    text_grad = by_batch(text_mine, text_theirs).astype(F32)
    second_grads = pull_second(
        scatter_rows(contract_cols(cross_grad_low[0], cross_q_full[0]) + contract_cols(cross_grad_low[1], cross_q_full[1]))
    )
    resid_one_grad = resid_two_grad + second_grads[0]
    grad_one_low = resid_one_grad.astype(BF)
    grad_one_all = gather_rows(grad_one_low)
    self_out_grad = reduce_last([contract_rows(p, grad_one_all) for p in mix_parts])
    mix_grad = to_heads([contract_cols(grad_one_all, w).astype(BF) for w in self_out_full], 1)[:, 0]
    q_back, k_back, v_back = attention_backward(query, key, value, self_sums, mix_grad)
    self_grads = pull_self(
        (q_back.astype(BF).astype(F32), k_back.astype(BF).astype(F32), v_back.astype(BF).astype(F32))
    )
    triple_low = from_heads(self_grads[0].astype(BF))
    triple_grad = reduce_first([contract_rows(normed_one_all, g) for g in triple_low])
    first_grads = pull_first(
        (
            resid_one_grad,
            scatter_rows(contract_cols(triple_low[0], triple_full[0]) + contract_cols(triple_low[1], triple_full[1])),
        )
    )
    summed_low = first_grads[0].astype(BF)
    summed_cols = lax.all_to_all(summed_low, "context", split_axis=1, concat_axis=0, tiled=True)
    skip_part = contract_rows(tok_all, summed_cols).reshape(2, nz, ny, -1, eb)
    keep = lax.dynamic_index_in_dim(skip_part, y, 2, keepdims=False)
    give = lax.dynamic_index_in_dim(skip_part, 1 - y, 2, keepdims=False)
    skip_total = (keep + other(give.astype(BF)).astype(F32)).astype(BF)
    skip_grad = lax.psum_scatter(jnp.transpose(skip_total, (1, 0, 2, 3)), "shard", scatter_dimension=0, tiled=True)[0]
    skip_grad_out = jnp.transpose(spread(skip_grad), (1, 2, 0, 3)).reshape(2, -1, width).astype(F32)

    skip_all = jnp.transpose(spread(skip_block), (1, 0, 2)).reshape(2 * width, width)
    both_low = by_batch(summed_low, other(summed_low)).reshape(batch * local_len, width)
    both_grad = contract_cols(both_low, skip_all).reshape(batch, local_len, 2, width)

    def place(parts, size, half, total):
        out = jnp.zeros(parts[0].shape[:-1] + (total,), F32)
        at = out.ndim - 1
        out = lax.dynamic_update_slice_in_dim(out, parts[0], y * half + k * size, at)
        return lax.dynamic_update_slice_in_dim(out, parts[1], (1 - y) * half + k * size, at)

    def col_sums(values, count=1):
        return jnp.sum(values.astype(F32), 0).reshape(count, -1)

    gains_grad = first_grads[2] + second_grads[1] + third_grads[1]
    biases_grad = first_grads[3] + second_grads[2] + third_grads[2]
    head_gain_grad = self_grads[1] + cross_grads[2]
    head_bias_grad = self_grads[2] + cross_grads[3]
    width_grad = jnp.stack(
        [
            jnp.sum(summed_low.astype(F32), 0),
            first_grads[1],
            jnp.sum(grad_one_low.astype(F32), 0),
            jnp.sum(grad_two_low.astype(F32), 0),
            jnp.sum(grad_out, 0),
        ]
    )
    column_parts = [
        jnp.concatenate([col_sums(t, 3), col_sums(c, 1), col_sums(p, 2)], 0)
        for t, c, p in zip(triple_low, cross_grad_low, pair_low)
    ]
    column_grad = place(column_parts, cb, half_cols, width)
    hidden_grad_sum = place([col_sums(h)[0] for h in hidden_grad], hb, half_hidden, hidden_biases.shape[0])
    shift_slots = lax.dynamic_update_slice_in_dim(
        jnp.zeros((sequences, width), F32), first_grads[1][None], z * ny + y, 0
    )
    vectors = lax.psum(
        (gains_grad, biases_grad, head_gain_grad, head_bias_grad, width_grad, column_grad, hidden_grad_sum, shift_slots),
        ("shard", "context", "tensor"),
    )
    shift_grad_out = lax.dot_general(
        silu_rows.astype(F32), vectors[7], (((0,), (0,)), ((), ())), precision=lax.Precision.HIGHEST
    )

    def spread_rows(values):
        return lax.all_gather(values, "context", axis=0, tiled=True).astype(F32)

    return (
        result_out,
        both_grad[:, :, 0],
        both_grad[:, :, 1],
        text_grad,
        skip_grad_out,
        shift_grad_out,
        spread_last(triple_grad, 3),
        spread_rows(self_out_grad),
        spread_last(cross_q_grad, 1)[:, 0],
        spread_last(cross_kv_grad, 2),
        spread_rows(cross_out_grad),
        spread_last(up_grad, 1)[:, 0],
        spread_rows(down_grad),
    ) + tuple(vectors[:7])


def solution(mesh):
    placed = (
        P("shard", "context", None),
        P("shard", "context", None),
        P("shard", None, None),
        P("shard", "context", None),
        P("shard"),
        P("shard", "context", None),
        P(None, ("shard", "tensor"), None),
        P(("shard", "tensor"), None),
        P("shard", None, "tensor"),
        P("tensor", "shard"),
        P("shard", "tensor"),
        P("shard", None, "tensor"),
        P("tensor", "shard"),
        P("shard", "tensor"),
        P("tensor", "shard"),
    ) + (P(),) * 7
    return jax.shard_map(
        on_device,
        mesh=mesh,
        in_specs=placed,
        out_specs=(
            P("shard", "context", None),
            P("shard", "context", None),
            P("shard", "context", None),
            P("shard", None, ("context", "tensor")),
        )
        + placed[6:15]
        + (P(),) * 7,
        check_vma=False,
    )
```

```python
import math

import jax
import jax.numpy as jnp
from jax import lax
from jax.sharding import PartitionSpec as P

epsilon = 1e-06
BF = jnp.bfloat16
F32 = jnp.float32


def matmul(left_side, right_side):
    return jnp.dot(left_side, right_side, preferred_element_type=F32)


def contract(form, left_side, right_side):
    return jnp.einsum(form, left_side, right_side, preferred_element_type=F32)


def contract_rows(left_side, right_side):
    return lax.dot_general(left_side, right_side, (((0,), (0,)), ((), ())), preferred_element_type=F32)


def contract_cols(left_side, right_side):
    return lax.dot_general(left_side, right_side, (((1,), (1,)), ((), ())), preferred_element_type=F32)


def layer_norm(values, scale_vec, offset):
    center = values - jnp.mean(values, -1, keepdims=True)
    spread = jnp.mean(center * center, -1, keepdims=True)
    return center * lax.rsqrt(spread + epsilon) * scale_vec + offset


def rotary_tables(grid_rows, head_size):
    quarter = head_size // 4
    frequencies = 1.0 / 10000.0 ** (jnp.arange(quarter, dtype=F32) * 2.0 / (head_size // 2))
    row_angle = grid_rows[:, 0:1].astype(F32) * frequencies
    col_angle = grid_rows[:, 1:2].astype(F32) * frequencies
    angles = jnp.concatenate([row_angle, row_angle, col_angle, col_angle], 1)
    return (jnp.cos(angles)[:, None, :], jnp.sin(angles)[:, None, :])


def rotate(values, cosine, sine_rows):
    quarter = values.shape[-1] // 4
    one = values[..., :quarter]
    two = values[..., quarter : 2 * quarter]
    three = values[..., 2 * quarter : 3 * quarter]
    four = values[..., 3 * quarter :]
    turned = jnp.concatenate([-two, one, -four, three], -1)
    return values * cosine + turned * sine_rows


def time_silu(stamps, model_width):
    half_width = model_width // 2
    frequencies = jnp.exp(-math.log(10000.0) * jnp.arange(half_width, dtype=F32) / half_width)
    angles = stamps.astype(F32)[:, None] * frequencies
    return jax.nn.silu(jnp.concatenate([jnp.cos(angles), jnp.sin(angles)], 1)).astype(BF)


def attention_forward(queries, key_rows, value_rows):
    score_scale = queries.shape[-1] ** (-0.5)
    scores = contract("qhd,khd->hqk", queries, key_rows) * score_scale
    row_max = jnp.max(scores, -1, keepdims=True)
    exponent = jnp.exp(scores - row_max)
    weight_sum = jnp.sum(exponent, -1, keepdims=True)
    weights_low = (exponent / weight_sum).astype(BF)
    mixture = contract("hqk,khd->qhd", weights_low, value_rows)
    return (mixture.astype(BF), (row_max + jnp.log(weight_sum))[..., 0])


def attention_backward(queries, key_rows, value_rows, log_sums, grad_mix):
    score_scale = queries.shape[-1] ** (-0.5)
    scores = contract("qhd,khd->hqk", queries, key_rows) * score_scale
    weights_full = jnp.exp(scores - log_sums[..., None])
    grad_weights = contract("qhd,khd->hqk", grad_mix, value_rows)
    inner = jnp.sum(weights_full * grad_weights, -1, keepdims=True)
    grad_scores = (weights_full * (grad_weights - inner)).astype(BF)
    query_grad = contract("hqk,khd->qhd", grad_scores, key_rows) * score_scale
    key_grad = contract("hqk,qhd->khd", grad_scores, queries) * score_scale
    value_grad = contract("hqk,qhd->khd", weights_full.astype(BF), grad_mix)
    return (query_grad, key_grad, value_grad)


def on_device(
    tokens, skip_in, text_in, grid_pos, time_ids, cotangent,
    skip_weight, shift_weight, triple_weight, self_out_weight, cross_q_weight,
    cross_kv_weight, cross_out_weight, up_weight, down_weight,
    norm_gains, norm_biases, head_gains, head_biases, width_biases, column_biases, hidden_biases,
):
    batch, local_len, width = tokens.shape
    text_len = text_in.shape[1]
    head_size = head_gains.shape[1]
    z = lax.axis_index("shard")
    k = lax.axis_index("context")
    y = lax.axis_index("tensor")
    nz, nk, ny = lax.axis_size("shard"), lax.axis_size("context"), lax.axis_size("tensor")
    assert batch == ny == 2
    rows_z = triple_weight.shape[0]
    half_cols = triple_weight.shape[2]
    half_hidden = up_weight.shape[1]
    cb = half_cols // nk
    hb = half_hidden // nk
    eb = width // nk
    hh = cb // head_size
    heads = ny * hh
    length = local_len * nk
    sequences = batch * nz
    swap = [(0, 1), (1, 0)]

    def mine(values):
        return lax.dynamic_index_in_dim(values, y, 0, keepdims=False)

    def block(values, size, axis):
        return lax.dynamic_slice_in_dim(values, k * size, size, axis)

    def other(values):
        return lax.ppermute(values, "tensor", swap)

    def pair(values):
        return (values, other(values))

    bits = [1 << i for i in range(nk.bit_length() - 1)]
    relative = jnp.arange(nk) ^ k

    def flip(values, axis_name, bit):
        count = lax.axis_size(axis_name)
        return lax.ppermute(values, axis_name, [(i, i ^ bit) for i in range(count)])

    def gather_rows(values):
        for bit in reversed(bits):
            values = jnp.concatenate([values, flip(values, "context", bit)], 0)
        return values

    order = [sum(((p >> j) & 1) << (len(bits) - 1 - j) for j in range(len(bits))) for p in range(nk)]

    def ranked(values, axis=0, back=False):
        where = (jnp.asarray(order) ^ k) if back else jnp.asarray(order)[relative]
        return jnp.take(values, where, axis=axis, indices_are_sorted=False, unique_indices=True)

    def scatter_rows(pieces):
        half = pieces[0][0].shape[0] // 2

        def part(first):
            total = None
            for left, right, form in pieces:
                now = form(left[:half] if first else left[half:], right)
                total = now if total is None else total + now
            return total

        sent = flip(part(False).astype(BF), "context", bits[0])
        total = part(True) + sent.astype(F32)
        for bit in bits[1:]:
            half = total.shape[0] // 2
            total = total[:half] + flip(total[half:].astype(BF), "context", bit).astype(F32)
        return total

    def by_batch(own, theirs):
        first = jnp.where(y == 0, own, theirs)
        second = jnp.where(y == 0, theirs, own)
        return jnp.stack([first, second])

    def gathered(values):
        return lax.all_gather(values, "shard", axis=0, tiled=True)

    pin = lax.optimization_barrier
    first_part = jnp.concatenate(
        [
            block(skip_weight, eb, 2).reshape(-1, eb),
            block(triple_weight, cb, 2).reshape(rows_z, 3 * cb),
            block(self_out_weight, cb, 0).T,
        ],
        1,
    )
    second_part = jnp.concatenate(
        [
            block(cross_q_weight, cb, 1),
            block(cross_kv_weight, cb, 2).reshape(rows_z, 2 * cb),
            block(cross_out_weight, cb, 0).T,
        ],
        1,
    )
    first_z = gathered(first_part)
    second_z = gathered(second_part)
    up_z = gathered(block(up_weight, hb, 1))
    down_z = gathered(block(down_weight, hb, 0).T)
    skip_z = first_z[:, :eb].reshape(nz, 2, -1, eb)
    skip_block = jnp.transpose(by_batch(skip_z, other(skip_z)), (2, 1, 0, 3, 4)).reshape(2 * width, eb)

    def own_columns(values, size, half):
        last = values.ndim - 1
        first = lax.dynamic_slice_in_dim(values, y * half + k * size, size, last)
        second = lax.dynamic_slice_in_dim(values, (1 - y) * half + k * size, size, last)
        return (first, second)

    tok_rows, skip_rows, cot_rows = mine(tokens), mine(skip_in), mine(cotangent)
    text_rows = mine(text_in)
    grid_all = gather_rows(mine(grid_pos))
    cosine, sine_rows = rotary_tables(grid_all, head_size)
    times = lax.all_to_all(jnp.broadcast_to(time_ids, (nz, batch)), "shard", 0, 0, tiled=True).reshape(-1)
    silu_all = time_silu(times, width)
    shift_rows_count = shift_weight.shape[0]
    silu_rows = lax.dynamic_slice_in_dim(silu_all, (z * ny + y) * shift_rows_count, shift_rows_count, 1)
    shift_part = matmul(silu_rows, shift_weight).reshape(nz, ny, width)
    shift_mine = lax.dynamic_index_in_dim(shift_part, y, 1, keepdims=False)
    shift_give = lax.dynamic_index_in_dim(shift_part, 1 - y, 1, keepdims=False)
    shift_part = shift_mine + other(shift_give)
    shift_row = jnp.sum(lax.all_to_all(shift_part, "shard", 0, 0, tiled=True), 0) + width_biases[1]

    tok_all = gather_rows(jnp.concatenate([tok_rows, skip_rows], 1))
    summed_block = ranked(matmul(tok_all, skip_block).astype(BF).reshape(nk, local_len, eb)).reshape(length, eb)
    summed = lax.all_to_all(summed_block, "context", split_axis=0, concat_axis=1, tiled=True).astype(F32) + width_biases[0]

    summed, first_z = pin((summed, first_z[:, eb:]))
    first_pair = pair(first_z)
    triple_full = [w[:, : 3 * cb] for w in first_pair]
    self_out_full = [w[:, 3 * cb :] for w in first_pair]

    def first_piece(summed_in, shift_in, gain_rows, bias_rows):
        resid_out = layer_norm(summed_in, gain_rows[0], bias_rows[0])
        return (resid_out, layer_norm(resid_out, gain_rows[1], bias_rows[1]) + shift_in)

    (resid_zero, normed_one), pull_first = jax.vjp(first_piece, summed, shift_row, norm_gains, norm_biases)
    normed_one_all = gather_rows(normed_one.astype(BF))
    triple_bias = own_columns(column_biases[0:3], cb, half_cols)

    def to_heads(parts, count):
        return jnp.concatenate([p.reshape(p.shape[0], count, hh, head_size) for p in parts], 2)

    def from_heads(values):
        rows, count = values.shape[0], values.shape[1]
        return (values[:, :, :hh].reshape(rows, count * cb), values[:, :, hh:].reshape(rows, count * cb))

    triple = to_heads([matmul(normed_one_all, w) + b.reshape(1, -1) for w, b in zip(triple_full, triple_bias)], 3)

    def self_piece(triple_in, gain_rows, bias_rows):
        queries = rotate(layer_norm(triple_in[:, 0], gain_rows[0], bias_rows[0]), cosine, sine_rows)
        key_rows = rotate(layer_norm(triple_in[:, 1], gain_rows[1], bias_rows[1]), cosine, sine_rows)
        return (queries, key_rows, triple_in[:, 2])

    (query, key, value), pull_self = jax.vjp(self_piece, triple, head_gains, head_biases)
    query, key, value = query.astype(BF), key.astype(BF), value.astype(BF)
    query, key, value, second_z = pin((query, key, value, second_z))
    second_pair = pair(second_z)
    cross_q_full = [w[:, :cb] for w in second_pair]
    cross_kv_full = [w[:, cb : 3 * cb] for w in second_pair]
    cross_out_full = [w[:, 3 * cb :] for w in second_pair]
    mix, self_sums = attention_forward(query, key, value)
    mix_parts = from_heads(mix[:, None])
    resid_one = resid_zero + (
        scatter_rows([(mix_parts[0], self_out_full[0], contract_cols), (mix_parts[1], self_out_full[1], contract_cols)]) + width_biases[2]
    )

    resid_one, up_z = pin((resid_one, up_z))
    up_full = pair(up_z)

    def second_piece(resid_in, gain_rows, bias_rows):
        return layer_norm(resid_in, gain_rows[2], bias_rows[2])

    normed_two, pull_second = jax.vjp(second_piece, resid_one, norm_gains, norm_biases)
    normed_two_all = gather_rows(normed_two.astype(BF))
    cq_bias = own_columns(column_biases[3], cb, half_cols)
    kv_bias = own_columns(column_biases[4:6], cb, half_cols)
    cross_raw = to_heads([matmul(normed_two_all, w) + b.reshape(1, -1) for w, b in zip(cross_q_full, cq_bias)], 1)
    pair_raw = to_heads([matmul(text_rows, w) + b.reshape(1, -1) for w, b in zip(cross_kv_full, kv_bias)], 2)

    def cross_piece(query_in, pair_in, gain_rows, bias_rows):
        queries = rotate(layer_norm(query_in[:, 0], gain_rows[2], bias_rows[2]), cosine, sine_rows)
        key_rows = layer_norm(pair_in[:, 0], gain_rows[3], bias_rows[3])
        return (queries, key_rows, pair_in[:, 1])

    (cq, ck, cv), pull_cross = jax.vjp(cross_piece, cross_raw, pair_raw, head_gains, head_biases)
    cq, ck, cv = cq.astype(BF), ck.astype(BF), cv.astype(BF)
    cq, ck, cv, down_z = pin((cq, ck, cv, down_z))
    down_full = pair(down_z)
    cross_mix, cross_sums = attention_forward(cq, ck, cv)
    cross_parts = from_heads(cross_mix[:, None])
    resid_two = resid_one + (
        scatter_rows([(cross_parts[0], cross_out_full[0], contract_cols), (cross_parts[1], cross_out_full[1], contract_cols)]) + width_biases[3]
    )

    def third_piece(resid_in, gain_rows, bias_rows):
        return layer_norm(resid_in, gain_rows[3], bias_rows[3])

    normed_three, pull_third = jax.vjp(third_piece, resid_two, norm_gains, norm_biases)
    normed_three_all = gather_rows(normed_three.astype(BF))
    hidden_bias = own_columns(hidden_biases, hb, half_hidden)

    def gelu_piece(hidden_in):
        return jax.nn.gelu(hidden_in, approximate=True)

    active, pull_gelu = [], []
    for w, b in zip(up_full, hidden_bias):
        act, pull = jax.vjp(gelu_piece, matmul(normed_three_all, w) + b)
        active.append(act.astype(BF))
        pull_gelu.append(pull)
    result = resid_two + (
        scatter_rows([(active[0], down_full[0], contract_cols), (active[1], down_full[1], contract_cols)]) + width_biases[4]
    )
    result_low = result.astype(BF)
    result_out = by_batch(result_low, other(result_low)).astype(F32)

    def reduced(own, theirs):
        total = own + other(theirs.astype(BF)).astype(F32)
        return lax.psum_scatter(total.astype(BF), "shard", scatter_dimension=0, tiled=True)

    def spread(values):
        return ranked(gather_rows(values[None]))

    def columns_out(values, count):
        got = values.reshape(nk, values.shape[1], count, -1)
        return jnp.transpose(got, (1, 2, 0, 3)).reshape(values.shape[1], count, -1).astype(F32)

    def rows_out(values):
        return jnp.transpose(values, (0, 2, 1)).reshape(-1, values.shape[1]).astype(F32)

    cot_all = gather_rows(cot_rows)
    grad_out = cot_rows.astype(F32)
    down_grad = spread(reduced(*[contract_rows(cot_all, a) for a in active]))
    hidden_grad = [pull(matmul(cot_all, w))[0].astype(BF) for pull, w in zip(pull_gelu, down_full)]
    up_grad = spread(reduced(*[contract_rows(normed_three_all, h) for h in hidden_grad]))
    third_grads = pull_third(
        scatter_rows([(hidden_grad[0], up_full[0], contract_cols), (hidden_grad[1], up_full[1], contract_cols)])
    )
    resid_two_grad = grad_out + third_grads[0]
    grad_two_low = resid_two_grad.astype(BF)
    grad_two_all = gather_rows(grad_two_low)
    cross_out_grad = [contract_rows(grad_two_all, p) for p in cross_parts]
    cross_mix_grad = to_heads([matmul(grad_two_all, w).astype(BF) for w in cross_out_full], 1)[:, 0]
    cq_back, ck_back, cv_back = attention_backward(cq, ck, cv, cross_sums, cross_mix_grad)
    cross_grads = pull_cross((cq_back, ck_back, cv_back))
    cross_grad_low = from_heads(cross_grads[0].astype(BF))
    pair_low = from_heads(cross_grads[1].astype(BF))
    cross_q_grad = [contract_rows(normed_two_all, g) for g in cross_grad_low]
    cross_kv_grad = [contract_rows(text_rows, g) for g in pair_low]
    text_part = contract_cols(pair_low[0], cross_kv_full[0]) + contract_cols(pair_low[1], cross_kv_full[1])
    text_part = lax.psum_scatter(text_part.astype(BF), "context", scatter_dimension=1, tiled=True)
    text_cols = text_part.shape[1] // ny
    text_mine = lax.dynamic_slice_in_dim(text_part, y * text_cols, text_cols, 1)
    text_theirs = other(lax.dynamic_slice_in_dim(text_part, (1 - y) * text_cols, text_cols, 1))
    text_grad = by_batch(text_mine, text_theirs).astype(F32)
    second_grads = pull_second(
        scatter_rows([(cross_grad_low[0], cross_q_full[0], contract_cols), (cross_grad_low[1], cross_q_full[1], contract_cols)])
    )
    resid_one_grad = resid_two_grad + second_grads[0]
    grad_one_low = resid_one_grad.astype(BF)
    grad_one_all = gather_rows(grad_one_low)
    self_out_grad = [contract_rows(grad_one_all, p) for p in mix_parts]
    small_grad = [jnp.concatenate(g, 1) for g in zip(cross_q_grad, cross_kv_grad, cross_out_grad, self_out_grad)]
    small_grad = spread(reduced(*small_grad))
    mix_grad = to_heads([matmul(grad_one_all, w).astype(BF) for w in self_out_full], 1)[:, 0]
    q_back, k_back, v_back = attention_backward(query, key, value, self_sums, mix_grad)
    self_grads = pull_self(
        (q_back.astype(BF).astype(F32), k_back.astype(BF).astype(F32), v_back.astype(BF).astype(F32))
    )
    triple_low = from_heads(self_grads[0].astype(BF))
    triple_grad = spread(reduced(*[contract_rows(normed_one_all, g) for g in triple_low]))
    first_grads = pull_first(
        (
            resid_one_grad,
            scatter_rows([(triple_low[0], triple_full[0], contract_cols), (triple_low[1], triple_full[1], contract_cols)]),
        )
    )
    summed_low = first_grads[0].astype(BF)
    summed_cols = lax.all_to_all(summed_low, "context", split_axis=1, concat_axis=0, tiled=True)
    summed_cols = ranked(summed_cols.reshape(nk, local_len, eb), 0, True).reshape(length, eb)
    skip_part = contract_rows(tok_all, summed_cols).reshape(2, nz, ny, -1, eb)
    keep = lax.dynamic_index_in_dim(skip_part, y, 2, keepdims=False)
    give = lax.dynamic_index_in_dim(skip_part, 1 - y, 2, keepdims=False)
    skip_total = (keep + other(give.astype(BF)).astype(F32)).astype(BF)
    skip_total = jnp.transpose(skip_total, (1, 0, 2, 3)).reshape(-1, eb)
    skip_grad = lax.psum_scatter(skip_total, "shard", scatter_dimension=0, tiled=True)
    skip_grad_out = jnp.transpose(spread(skip_grad), (1, 0, 2)).reshape(2, -1, width).astype(F32)

    skip_all = gather_rows(skip_block[None])
    both_low = by_batch(summed_low, other(summed_low)).reshape(batch * local_len, nk, eb)
    both_grad = contract("tke,kde->td", ranked(both_low, 1, True), skip_all).reshape(batch, local_len, 2, width)

    def place(parts, size, half, total):
        out = jnp.zeros(parts[0].shape[:-1] + (total,), F32)
        at = out.ndim - 1
        out = lax.dynamic_update_slice_in_dim(out, parts[0], y * half + k * size, at)
        return lax.dynamic_update_slice_in_dim(out, parts[1], (1 - y) * half + k * size, at)

    def everywhere(parts):
        flat = jnp.concatenate([p.reshape(-1) for p in parts])
        size = flat.shape[0]
        flat = jnp.pad(flat, (0, -size % 1024)).reshape(-1, 128)
        for axis_name in ("context", "tensor", "shard"):
            for i in range(lax.axis_size(axis_name).bit_length() - 1):
                flat = flat + flip(flat, axis_name, 1 << i)
        flat, out, at = flat.reshape(-1), [], 0
        for p in parts:
            out.append(flat[at : at + p.size].reshape(p.shape))
            at += p.size
        return out

    def col_sums(values, count=1):
        return jnp.sum(values.astype(F32), 0).reshape(count, -1)

    gains_grad = first_grads[2] + second_grads[1] + third_grads[1]
    biases_grad = first_grads[3] + second_grads[2] + third_grads[2]
    head_gain_grad = self_grads[1] + cross_grads[2]
    head_bias_grad = self_grads[2] + cross_grads[3]
    width_grad = jnp.stack(
        [
            jnp.sum(summed_low.astype(F32), 0),
            first_grads[1],
            jnp.sum(grad_one_low.astype(F32), 0),
            jnp.sum(grad_two_low.astype(F32), 0),
            jnp.sum(grad_out, 0),
        ]
    )
    column_parts = [
        jnp.concatenate([col_sums(t, 3), col_sums(c, 1), col_sums(p, 2)], 0)
        for t, c, p in zip(triple_low, cross_grad_low, pair_low)
    ]
    column_grad = place(column_parts, cb, half_cols, width)
    hidden_grad_sum = place([col_sums(h)[0] for h in hidden_grad], hb, half_hidden, hidden_biases.shape[0])
    shift_slots = lax.dynamic_update_slice_in_dim(
        jnp.zeros((sequences, width), F32), first_grads[1][None], z * ny + y, 0
    )
    vectors = everywhere(
        (gains_grad, biases_grad, head_gain_grad, head_bias_grad, width_grad, column_grad, hidden_grad_sum, shift_slots)
    )
    shift_grad_out = lax.dot_general(
        silu_rows.astype(F32), vectors[7], (((0,), (0,)), ((), ())), precision=lax.Precision.HIGHEST
    )

    return (
        result_out,
        both_grad[:, :, 0],
        both_grad[:, :, 1],
        text_grad,
        skip_grad_out,
        shift_grad_out,
        columns_out(triple_grad, 3),
        rows_out(small_grad[:, :, 4 * cb :]),
        columns_out(small_grad[:, :, :cb], 1)[:, 0],
        columns_out(small_grad[:, :, cb : 3 * cb], 2),
        rows_out(small_grad[:, :, 3 * cb : 4 * cb]),
        columns_out(up_grad, 1)[:, 0],
        rows_out(down_grad),
    ) + tuple(vectors[:7])


def solution(mesh):
    placed = (
        P("shard", "context", None),
        P("shard", "context", None),
        P("shard", None, None),
        P("shard", "context", None),
        P("shard"),
        P("shard", "context", None),
        P(None, ("shard", "tensor"), None),
        P(("shard", "tensor"), None),
        P("shard", None, "tensor"),
        P("tensor", "shard"),
        P("shard", "tensor"),
        P("shard", None, "tensor"),
        P("tensor", "shard"),
        P("shard", "tensor"),
        P("tensor", "shard"),
    ) + (P(),) * 7
    return jax.shard_map(
        on_device,
        mesh=mesh,
        in_specs=placed,
        out_specs=(
            P("shard", "context", None),
            P("shard", "context", None),
            P("shard", "context", None),
            P("shard", None, ("context", "tensor")),
        )
        + placed[6:15]
        + (P(),) * 7,
        check_vma=False,
    )
```

```python
import math

import jax
import jax.numpy as jnp
from jax import lax
from jax.sharding import PartitionSpec as P

epsilon = 1e-06
BF = jnp.bfloat16
F32 = jnp.float32


def matmul(left_side, right_side):
    return jnp.dot(left_side, right_side, preferred_element_type=F32)


def contract(form, left_side, right_side):
    return jnp.einsum(form, left_side, right_side, preferred_element_type=F32)


def contract_rows(left_side, right_side):
    return lax.dot_general(left_side, right_side, (((0,), (0,)), ((), ())), preferred_element_type=F32)


def contract_cols(left_side, right_side):
    return lax.dot_general(left_side, right_side, (((1,), (1,)), ((), ())), preferred_element_type=F32)


def layer_norm(values, scale_vec, offset):
    center = values - jnp.mean(values, -1, keepdims=True)
    spread = jnp.mean(center * center, -1, keepdims=True)
    return center * lax.rsqrt(spread + epsilon) * scale_vec + offset


def rotary_tables(grid_rows, head_size):
    quarter = head_size // 4
    frequencies = 1.0 / 10000.0 ** (jnp.arange(quarter, dtype=F32) * 2.0 / (head_size // 2))
    row_angle = grid_rows[:, 0:1].astype(F32) * frequencies
    col_angle = grid_rows[:, 1:2].astype(F32) * frequencies
    angles = jnp.concatenate([row_angle, row_angle, col_angle, col_angle], 1)
    return (jnp.cos(angles)[:, None, :], jnp.sin(angles)[:, None, :])


def rotate(values, cosine, sine_rows):
    quarter = values.shape[-1] // 4
    one = values[..., :quarter]
    two = values[..., quarter : 2 * quarter]
    three = values[..., 2 * quarter : 3 * quarter]
    four = values[..., 3 * quarter :]
    turned = jnp.concatenate([-two, one, -four, three], -1)
    return values * cosine + turned * sine_rows


def time_silu(stamps, model_width):
    half_width = model_width // 2
    frequencies = jnp.exp(-math.log(10000.0) * jnp.arange(half_width, dtype=F32) / half_width)
    angles = stamps.astype(F32)[:, None] * frequencies
    return jax.nn.silu(jnp.concatenate([jnp.cos(angles), jnp.sin(angles)], 1)).astype(BF)


def attention_forward(queries, key_rows, value_rows):
    score_scale = queries.shape[-1] ** (-0.5)
    scores = contract("qhd,khd->hqk", queries, key_rows) * score_scale
    row_max = jnp.max(scores, -1, keepdims=True)
    exponent = jnp.exp(scores - row_max)
    weight_sum = jnp.sum(exponent, -1, keepdims=True)
    weights_low = (exponent / weight_sum).astype(BF)
    mixture = contract("hqk,khd->qhd", weights_low, value_rows)
    return (mixture.astype(BF), (row_max + jnp.log(weight_sum))[..., 0])


def attention_backward(queries, key_rows, value_rows, log_sums, grad_mix):
    score_scale = queries.shape[-1] ** (-0.5)
    scores = contract("qhd,khd->hqk", queries, key_rows) * score_scale
    weights_full = jnp.exp(scores - log_sums[..., None])
    grad_weights = contract("qhd,khd->hqk", grad_mix, value_rows)
    inner = jnp.sum(weights_full * grad_weights, -1, keepdims=True)
    grad_scores = (weights_full * (grad_weights - inner)).astype(BF)
    query_grad = contract("hqk,khd->qhd", grad_scores, key_rows) * score_scale
    key_grad = contract("hqk,qhd->khd", grad_scores, queries) * score_scale
    value_grad = contract("hqk,qhd->khd", weights_full.astype(BF), grad_mix)
    return (query_grad, key_grad, value_grad)


def on_device(
    tokens, skip_in, text_in, grid_pos, time_ids, cotangent,
    skip_weight, shift_weight, triple_weight, self_out_weight, cross_q_weight,
    cross_kv_weight, cross_out_weight, up_weight, down_weight,
    norm_gains, norm_biases, head_gains, head_biases, width_biases, column_biases, hidden_biases,
):
    batch, local_len, width = tokens.shape
    text_len = text_in.shape[1]
    head_size = head_gains.shape[1]
    z = lax.axis_index("shard")
    k = lax.axis_index("context")
    y = lax.axis_index("tensor")
    nz, nk, ny = lax.axis_size("shard"), lax.axis_size("context"), lax.axis_size("tensor")
    assert batch == ny == 2
    rows_z = triple_weight.shape[0]
    half_cols = triple_weight.shape[2]
    half_hidden = up_weight.shape[1]
    cb = half_cols // nk
    hb = half_hidden // nk
    eb = width // nk
    hh = cb // head_size
    heads = ny * hh
    length = local_len * nk
    sequences = batch * nz
    swap = [(0, 1), (1, 0)]

    def mine(values):
        return lax.dynamic_index_in_dim(values, y, 0, keepdims=False)

    def block(values, size, axis):
        return lax.dynamic_slice_in_dim(values, k * size, size, axis)

    def other(values):
        return lax.ppermute(values, "tensor", swap)

    bits = [1 << i for i in range(nk.bit_length() - 1)]
    relative = jnp.arange(nk) ^ k

    def flip(values, axis_name, bit):
        count = lax.axis_size(axis_name)
        return lax.ppermute(values, axis_name, [(i, i ^ bit) for i in range(count)])

    def gather_far(values):
        for bit in reversed(bits[1:]):
            values = jnp.concatenate([values, flip(values, "context", bit)], 0)
        return values

    def gather_near(values):
        return jnp.concatenate([values, flip(values, "context", bits[0])], 0)

    def gather_rows(values):
        return gather_near(gather_far(values))

    order = [sum(((p >> j) & 1) << (len(bits) - 1 - j) for j in range(len(bits))) for p in range(nk)]

    def ranked(values, axis=0, back=False):
        where = (jnp.asarray(order) ^ k) if back else jnp.asarray(order)[relative]
        return jnp.take(values, where, axis=axis, indices_are_sorted=False, unique_indices=True)

    def scatter_rows(pieces):
        half = pieces[0][0].shape[0] // 2

        def part(first):
            total = None
            for left, right, form in pieces:
                now = form(left[:half] if first else left[half:], right)
                total = now if total is None else total + now
            return total

        sent = flip(part(False).astype(BF), "context", bits[0])
        total = part(True) + sent.astype(F32)
        for bit in bits[1:]:
            half = total.shape[0] // 2
            total = total[:half] + flip(total[half:].astype(BF), "context", bit).astype(F32)
        return total

    def by_batch(own, theirs):
        first = jnp.where(y == 0, own, theirs)
        second = jnp.where(y == 0, theirs, own)
        return jnp.stack([first, second])

    def gathered(values):
        return lax.all_gather(values, ("tensor", "shard"), axis=0, tiled=True)

    def halves(values):
        return (values[:width], values[width:])

    pin = lax.optimization_barrier
    first_part = jnp.concatenate(
        [
            block(triple_weight, cb, 2).reshape(rows_z, 3 * cb),
            block(self_out_weight, cb, 0).T,
        ],
        1,
    )
    second_part = jnp.concatenate(
        [
            block(cross_q_weight, cb, 1),
            block(cross_kv_weight, cb, 2).reshape(rows_z, 2 * cb),
            block(cross_out_weight, cb, 0).T,
        ],
        1,
    )
    skip_part = jnp.pad(block(skip_weight, eb, 2).reshape(-1, eb), ((0, 0), (0, -eb % 128)))
    skip_z = lax.all_gather(skip_part, ("shard", "tensor"), axis=0, tiled=True)
    skip_block = jnp.transpose(skip_z[:, :eb].reshape(nz * ny, 2, -1, eb), (1, 0, 2, 3)).reshape(2 * width, eb)
    first_z = gathered(first_part)
    second_z = gathered(second_part)
    up_z = gathered(block(up_weight, hb, 1))
    down_z = gathered(block(down_weight, hb, 0).T)

    def own_columns(values, size, half):
        last = values.ndim - 1
        first = lax.dynamic_slice_in_dim(values, k * size, size, last)
        second = lax.dynamic_slice_in_dim(values, half + k * size, size, last)
        return (first, second)

    tok_rows, skip_rows, cot_rows = mine(tokens), mine(skip_in), mine(cotangent)
    text_rows = mine(text_in)
    grid_all = gather_rows(mine(grid_pos))
    cosine, sine_rows = rotary_tables(grid_all, head_size)
    times = lax.all_to_all(jnp.broadcast_to(time_ids, (nz, batch)), "shard", 0, 0, tiled=True).reshape(-1)
    silu_all = time_silu(times, width)
    shift_rows_count = shift_weight.shape[0]
    silu_rows = lax.dynamic_slice_in_dim(silu_all, (z * ny + y) * shift_rows_count, shift_rows_count, 1)
    shift_part = matmul(silu_rows, shift_weight).reshape(nz, ny, width)
    shift_mine = lax.dynamic_index_in_dim(shift_part, y, 1, keepdims=False)
    shift_give = lax.dynamic_index_in_dim(shift_part, 1 - y, 1, keepdims=False)
    shift_got = other(shift_give)
    shift_part = shift_mine + shift_got
    shift_row = jnp.sum(lax.all_to_all(shift_part, "shard", 0, 0, tiled=True), 0) + width_biases[1]

    tok_here = gather_far(jnp.concatenate([tok_rows, skip_rows], 1))
    tok_halves = pin((tok_here, flip(tok_here, "context", bits[0])))
    summed_block = jnp.concatenate([matmul(t, skip_block).astype(BF) for t in tok_halves], 0)
    summed_block = ranked(summed_block.reshape(nk, local_len, eb)).reshape(length, eb)
    summed = lax.all_to_all(summed_block, "context", split_axis=0, concat_axis=1, tiled=True).astype(F32) + width_biases[0]

    first_pair = halves(first_z)
    triple_full = [w[:, : 3 * cb] for w in first_pair]
    self_out_full = [w[:, 3 * cb :] for w in first_pair]

    def first_piece(summed_in, shift_in, gain_rows, bias_rows):
        resid_out = layer_norm(summed_in, gain_rows[0], bias_rows[0])
        return (resid_out, layer_norm(resid_out, gain_rows[1], bias_rows[1]) + shift_in)

    (resid_zero, normed_one), pull_first = jax.vjp(first_piece, summed, shift_row, norm_gains, norm_biases)
    normed_one_all = gather_rows(normed_one.astype(BF))
    triple_bias = own_columns(column_biases[0:3], cb, half_cols)

    def to_heads(parts, count):
        return jnp.concatenate([p.reshape(p.shape[0], count, hh, head_size) for p in parts], 2)

    def from_heads(values):
        rows, count = values.shape[0], values.shape[1]
        return (values[:, :, :hh].reshape(rows, count * cb), values[:, :, hh:].reshape(rows, count * cb))

    triple = to_heads([matmul(normed_one_all, w) + b.reshape(1, -1) for w, b in zip(triple_full, triple_bias)], 3)

    def self_piece(triple_in, gain_rows, bias_rows):
        queries = rotate(layer_norm(triple_in[:, 0], gain_rows[0], bias_rows[0]), cosine, sine_rows)
        key_rows = rotate(layer_norm(triple_in[:, 1], gain_rows[1], bias_rows[1]), cosine, sine_rows)
        return (queries, key_rows, triple_in[:, 2])

    (query, key, value), pull_self = jax.vjp(self_piece, triple, head_gains, head_biases)
    query, key, value = query.astype(BF), key.astype(BF), value.astype(BF)
    query, key, value, cot_late = pin((query, key, value, cot_rows))
    cot_far = gather_far(cot_late)
    mix, self_sums = attention_forward(query, key, value)
    mix, cot_far = pin((mix, cot_far))
    mix_parts = from_heads(mix[:, None])
    resid_one = resid_zero + (
        scatter_rows([(mix_parts[0], self_out_full[0], contract_cols), (mix_parts[1], self_out_full[1], contract_cols)]) + width_biases[2]
    )


    resid_one, second_z = pin((resid_one, second_z))

    def second_piece(resid_in, gain_rows, bias_rows):
        return layer_norm(resid_in, gain_rows[2], bias_rows[2])

    normed_two, pull_second = jax.vjp(second_piece, resid_one, norm_gains, norm_biases)
    second_pair = halves(second_z)
    cross_q_full = [w[:, :cb] for w in second_pair]
    cross_kv_full = [w[:, cb : 3 * cb] for w in second_pair]
    cross_out_full = [w[:, 3 * cb :] for w in second_pair]
    normed_two_all = gather_rows(normed_two.astype(BF))
    cq_bias = own_columns(column_biases[3], cb, half_cols)
    kv_bias = own_columns(column_biases[4:6], cb, half_cols)
    cross_raw = to_heads([matmul(normed_two_all, w) + b.reshape(1, -1) for w, b in zip(cross_q_full, cq_bias)], 1)
    pair_raw = to_heads([matmul(text_rows, w) + b.reshape(1, -1) for w, b in zip(cross_kv_full, kv_bias)], 2)

    def cross_piece(query_in, pair_in, gain_rows, bias_rows):
        queries = rotate(layer_norm(query_in[:, 0], gain_rows[2], bias_rows[2]), cosine, sine_rows)
        key_rows = layer_norm(pair_in[:, 0], gain_rows[3], bias_rows[3])
        return (queries, key_rows, pair_in[:, 1])

    (cq, ck, cv), pull_cross = jax.vjp(cross_piece, cross_raw, pair_raw, head_gains, head_biases)
    cq, ck, cv = cq.astype(BF), ck.astype(BF), cv.astype(BF)
    cross_mix, cross_sums = attention_forward(cq, ck, cv)
    cross_parts = from_heads(cross_mix[:, None])
    resid_two = resid_one + (
        scatter_rows([(cross_parts[0], cross_out_full[0], contract_cols), (cross_parts[1], cross_out_full[1], contract_cols)]) + width_biases[3]
    )

    resid_two, up_z = pin((resid_two, up_z))

    def third_piece(resid_in, gain_rows, bias_rows):
        return layer_norm(resid_in, gain_rows[3], bias_rows[3])

    normed_three, pull_third = jax.vjp(third_piece, resid_two, norm_gains, norm_biases)
    normed_three_all = gather_rows(normed_three.astype(BF))
    up_full, down_full = halves(up_z), halves(down_z)
    normed_three_all, skip_late = pin((normed_three_all, skip_block))
    skip_far = gather_far(skip_late[None])
    hidden_bias = own_columns(hidden_biases, hb, half_hidden)

    def gelu_piece(hidden_in):
        return jax.nn.gelu(hidden_in, approximate=True)

    active, pull_gelu = [], []
    for w, b in zip(up_full, hidden_bias):
        act, pull = jax.vjp(gelu_piece, matmul(normed_three_all, w) + b)
        active.append(act.astype(BF))
        pull_gelu.append(pull)
    def reduced(parts):
        total = jnp.concatenate([p.astype(BF) for p in parts], 0)
        return lax.psum_scatter(total, ("tensor", "shard"), scatter_dimension=0, tiled=True)

    def own_first(parts):
        return (jnp.where(y == 0, parts[0], parts[1]), jnp.where(y == 0, parts[1], parts[0]))

    def over_shard(own, received):
        total = own + received.astype(F32)
        return lax.psum_scatter(total.astype(BF), "shard", scatter_dimension=0, tiled=True)

    def spread(values):
        values = values[None]
        for bit in reversed(bits):
            got, high = flip(values, "context", bit), (k & bit) != 0
            values = jnp.concatenate([jnp.where(high, got, values), jnp.where(high, values, got)], 0)
        return values

    def by_rank(values, count):
        depth = len(bits)
        rows = values.shape[1]
        values = values.reshape((2,) * depth + (rows, count, -1))
        back = tuple(reversed(range(depth)))
        return jnp.transpose(values, (depth, depth + 1) + back + (depth + 2,)).reshape(rows, count, -1)

    def columns_out(values, count):
        return by_rank(spread(values), count).astype(F32)

    def placed_out(values, count):
        got = gather_rows(values[None])
        size = values.shape[1] // count
        source = ((jnp.asarray(order) ^ k)[:, None] * size + jnp.arange(size)).astype(jnp.int32)
        select = (source[:, :, None] == jnp.arange(nk * size)).astype(BF)
        return jnp.stack(
            [contract("prn,pnm->rm", got[:, :, i * size : (i + 1) * size], select) for i in range(count)], 1
        )

    def rows_out(values):
        depth = len(bits)
        count, rows = values.shape[1:]
        values = values.reshape((2,) * depth + (count, rows))
        values = jnp.transpose(values, tuple(reversed(range(depth))) + (depth, depth + 1))
        return values.reshape(-1, rows).astype(F32)

    def wide_out(values):
        return jnp.concatenate([values[order[p]] for p in range(nk)], 1).astype(F32)

    cot_all = gather_near(cot_far)
    grad_out = cot_rows.astype(F32)
    down_grad = reduced([contract_rows(cot_all, a) for a in active]).T
    hidden_grad = [pull(matmul(cot_all, w))[0].astype(BF) for pull, w in zip(pull_gelu, down_full)]
    hidden_grad[0], hidden_grad[1], skip_far = pin((hidden_grad[0], hidden_grad[1], skip_far))
    skip_all = gather_near(skip_far)
    up_grad = reduced([contract_rows(normed_three_all, h) for h in hidden_grad])
    third_grads = pull_third(
        scatter_rows([(hidden_grad[0], up_full[0], contract_cols), (hidden_grad[1], up_full[1], contract_cols)])
    )
    resid_two_grad = grad_out + third_grads[0]
    grad_two_low = resid_two_grad.astype(BF)
    grad_two_all = gather_rows(grad_two_low)
    cross_out_grad = [contract_rows(grad_two_all, p) for p in cross_parts]
    cross_mix_grad = to_heads([matmul(grad_two_all, w).astype(BF) for w in cross_out_full], 1)[:, 0]
    cq_back, ck_back, cv_back = attention_backward(cq, ck, cv, cross_sums, cross_mix_grad)
    cross_grads = pull_cross((cq_back, ck_back, cv_back))
    cross_grad_low = from_heads(cross_grads[0].astype(BF))
    pair_low = from_heads(cross_grads[1].astype(BF))
    cross_q_grad = [contract_rows(normed_two_all, g) for g in cross_grad_low]
    cross_kv_grad = [contract_rows(text_rows, g) for g in pair_low]
    text_part = contract_cols(pair_low[0], cross_kv_full[0]) + contract_cols(pair_low[1], cross_kv_full[1])
    text_part = lax.psum_scatter(text_part.astype(BF), "context", scatter_dimension=1, tiled=True)
    text_cols = text_part.shape[1] // ny
    text_mine = lax.dynamic_slice_in_dim(text_part, y * text_cols, text_cols, 1)
    text_theirs = other(lax.dynamic_slice_in_dim(text_part, (1 - y) * text_cols, text_cols, 1))
    text_grad = by_batch(text_mine, text_theirs).astype(F32)
    second_grads = pull_second(
        scatter_rows([(cross_grad_low[0], cross_q_full[0], contract_cols), (cross_grad_low[1], cross_q_full[1], contract_cols)])
    )
    resid_one_grad = resid_two_grad + second_grads[0]
    grad_one_low = resid_one_grad.astype(BF)
    grad_one_all = gather_rows(grad_one_low)
    self_out_grad = [contract_rows(grad_one_all, p) for p in mix_parts]
    small_grad = [jnp.concatenate(g, 1) for g in zip(cross_q_grad, cross_kv_grad, cross_out_grad, self_out_grad)]
    small_grad = own_first(small_grad)
    mix_grad = to_heads([matmul(grad_one_all, w).astype(BF) for w in self_out_full], 1)[:, 0]
    mix_grad, small_low, down_grad, active[0], active[1] = pin(
        (mix_grad, small_grad[1].astype(BF), down_grad, active[0], active[1])
    )
    down_grad = spread(down_grad)
    small_low = other(small_low)
    result = resid_two + (
        scatter_rows([(active[0], down_full[0], contract_cols), (active[1], down_full[1], contract_cols)]) + width_biases[4]
    )
    result_low = result.astype(BF)
    result_out = by_batch(result_low, other(result_low)).astype(F32)
    q_back, k_back, v_back = attention_backward(query, key, value, self_sums, mix_grad)
    q_back, k_back, v_back = q_back.astype(BF), k_back.astype(BF), v_back.astype(BF)
    self_grads = pull_self(
        (q_back.astype(F32), k_back.astype(F32), v_back.astype(F32))
    )
    triple_raw, small_low = pin((self_grads[0].astype(BF), small_low))
    small_grad = over_shard(small_grad[0], small_low)
    triple_low = from_heads(triple_raw)
    triple_grad = [contract_rows(normed_one_all, g) for g in own_first(triple_low)]
    triple_got = other(triple_grad[1].astype(BF))
    normed_grad = scatter_rows([(triple_low[0], triple_full[0], contract_cols), (triple_low[1], triple_full[1], contract_cols)])
    normed_grad, triple_got, up_grad = pin((normed_grad, triple_got, up_grad))
    up_grad = spread(up_grad)
    triple_grad = over_shard(triple_grad[0], triple_got)
    first_grads = pull_first((resid_one_grad, normed_grad))
    summed_low = first_grads[0].astype(BF)
    summed_cols = lax.all_to_all(summed_low, "context", split_axis=1, concat_axis=0, tiled=True)
    summed_cols = ranked(summed_cols.reshape(nk, local_len, eb), 0, True).reshape(length, eb)
    skip_part = contract_rows(tok_halves[0], summed_cols[: length // 2]) + contract_rows(tok_halves[1], summed_cols[length // 2 :])
    skip_part = pin(skip_part.astype(BF)).reshape(2, nz, ny, -1, eb)
    keep = lax.dynamic_index_in_dim(skip_part, y, 2, keepdims=False)
    give = lax.dynamic_index_in_dim(skip_part, 1 - y, 2, keepdims=False)
    skip_total = (keep.astype(F32) + other(give).astype(F32)).astype(BF)
    skip_total = jnp.transpose(skip_total, (1, 0, 2, 3)).reshape(-1, eb)
    skip_grad = lax.psum_scatter(skip_total, "shard", scatter_dimension=0, tiled=True)
    skip_grad_out = placed_out(skip_grad, 1).reshape(2, -1, width)

    both_low = by_batch(summed_low, other(summed_low)).reshape(batch * local_len, nk, eb)
    both_low = ranked(both_low, 1, True)
    tok_grad, skip_rows_grad = [
        contract("tke,kde->td", both_low, w).reshape(batch, local_len, width)
        for w in (skip_all[:, :width], skip_all[:, width:])
    ]

    def place(parts, size, half, total):
        out = jnp.zeros(parts[0].shape[:-1] + (total,), F32)
        at = out.ndim - 1
        out = lax.dynamic_update_slice_in_dim(out, parts[0], k * size, at)
        return lax.dynamic_update_slice_in_dim(out, parts[1], half + k * size, at)

    def everywhere(parts):
        flat = jnp.concatenate([p.reshape(-1) for p in parts])
        flat = pin((flat, skip_part))[0]
        size = flat.shape[0]
        flat = jnp.pad(flat, (0, -size % 1024)).reshape(-1, 128)
        for axis_name in ("context", "tensor", "shard"):
            for i in range(lax.axis_size(axis_name).bit_length() - 1):
                flat = flat + flip(flat, axis_name, 1 << i)
        flat, out, at = flat.reshape(-1), [], 0
        for p in parts:
            out.append(flat[at : at + p.size].reshape(p.shape))
            at += p.size
        return out

    def col_sums(values, count=1):
        return jnp.sum(values.astype(F32), 0).reshape(count, -1)

    gains_grad = first_grads[2] + second_grads[1] + third_grads[1]
    biases_grad = first_grads[3] + second_grads[2] + third_grads[2]
    head_gain_grad = self_grads[1] + cross_grads[2]
    head_bias_grad = self_grads[2] + cross_grads[3]
    width_grad = jnp.stack(
        [
            jnp.sum(summed_low.astype(F32), 0),
            first_grads[1],
            jnp.sum(grad_one_low.astype(F32), 0),
            jnp.sum(grad_two_low.astype(F32), 0),
            jnp.sum(grad_out, 0),
        ]
    )
    column_parts = [
        jnp.concatenate([col_sums(t, 3), col_sums(c, 1), col_sums(p, 2)], 0)
        for t, c, p in zip(triple_low, cross_grad_low, pair_low)
    ]
    column_grad = place(column_parts, cb, half_cols, width)
    hidden_grad_sum = place([col_sums(h)[0] for h in hidden_grad], hb, half_hidden, hidden_biases.shape[0])
    shift_slots = lax.dynamic_update_slice_in_dim(
        jnp.zeros((sequences, width), F32), first_grads[1][None], z * ny + y, 0
    )
    vectors = everywhere(
        (gains_grad, biases_grad, head_gain_grad, head_bias_grad, width_grad, column_grad, hidden_grad_sum, shift_slots)
    )
    shift_grad_out = lax.dot_general(
        silu_rows.astype(F32), vectors[7], (((0,), (0,)), ((), ())), precision=lax.Precision.HIGHEST
    )

    return (
        result_out,
        tok_grad,
        skip_rows_grad,
        text_grad,
        skip_grad_out,
        shift_grad_out,
        placed_out(triple_grad, 3),
        rows_out(spread(small_grad[:, 4 * cb :].T)),
        placed_out(small_grad[:, :cb], 1)[:, 0],
        placed_out(small_grad[:, cb : 3 * cb], 2),
        rows_out(spread(small_grad[:, 3 * cb : 4 * cb].T)),
        wide_out(up_grad),
        rows_out(down_grad),
    ) + tuple(vectors[:7])


def solution(mesh):
    placed = (
        P("shard", "context", None),
        P("shard", "context", None),
        P("shard", None, None),
        P("shard", "context", None),
        P("shard"),
        P("shard", "context", None),
        P(None, ("shard", "tensor"), None),
        P(("shard", "tensor"), None),
        P("shard", None, "tensor"),
        P("tensor", "shard"),
        P("shard", "tensor"),
        P("shard", None, "tensor"),
        P("tensor", "shard"),
        P("shard", "tensor"),
        P("tensor", "shard"),
    ) + (P(),) * 7
    return jax.shard_map(
        on_device,
        mesh=mesh,
        in_specs=placed,
        out_specs=(
            P("shard", "context", None),
            P("shard", "context", None),
            P("shard", "context", None),
            P("shard", None, ("context", "tensor")),
        )
        + placed[6:15]
        + (P(),) * 7,
        check_vma=False,
    )
```

```python
import math

import jax
import jax.numpy as jnp
from jax import lax
from jax.sharding import PartitionSpec as P

epsilon = 1e-06
BF = jnp.bfloat16
F32 = jnp.float32


def matmul(left_side, right_side):
    return jnp.dot(left_side, right_side, preferred_element_type=F32)


def contract(form, left_side, right_side):
    return jnp.einsum(form, left_side, right_side, preferred_element_type=F32)


def contract_rows(left_side, right_side):
    return lax.dot_general(left_side, right_side, (((0,), (0,)), ((), ())), preferred_element_type=F32)


def contract_cols(left_side, right_side):
    return lax.dot_general(left_side, right_side, (((1,), (1,)), ((), ())), preferred_element_type=F32)


def layer_norm(values, scale_vec, offset):
    center = values - jnp.mean(values, -1, keepdims=True)
    spread = jnp.mean(center * center, -1, keepdims=True)
    return center * lax.rsqrt(spread + epsilon) * scale_vec + offset


def rotary_tables(grid_rows, head_size):
    quarter = head_size // 4
    frequencies = 1.0 / 10000.0 ** (jnp.arange(quarter, dtype=F32) * 2.0 / (head_size // 2))
    row_angle = grid_rows[:, 0:1].astype(F32) * frequencies
    col_angle = grid_rows[:, 1:2].astype(F32) * frequencies
    angles = jnp.concatenate([row_angle, row_angle, col_angle, col_angle], 1)
    return (jnp.cos(angles)[:, None, :], jnp.sin(angles)[:, None, :])


def rotate(values, cosine, sine_rows):
    quarter = values.shape[-1] // 4
    one = values[..., :quarter]
    two = values[..., quarter : 2 * quarter]
    three = values[..., 2 * quarter : 3 * quarter]
    four = values[..., 3 * quarter :]
    turned = jnp.concatenate([-two, one, -four, three], -1)
    return values * cosine + turned * sine_rows


def time_silu(stamps, model_width):
    half_width = model_width // 2
    frequencies = jnp.exp(-math.log(10000.0) * jnp.arange(half_width, dtype=F32) / half_width)
    angles = stamps.astype(F32)[:, None] * frequencies
    return jax.nn.silu(jnp.concatenate([jnp.cos(angles), jnp.sin(angles)], 1)).astype(BF)


def attention_forward(queries, key_rows, value_rows):
    score_scale = queries.shape[-1] ** (-0.5)
    scores = contract("qhd,khd->hqk", queries, key_rows) * score_scale
    row_max = jnp.max(scores, -1, keepdims=True)
    exponent = jnp.exp(scores - row_max)
    weight_sum = jnp.sum(exponent, -1, keepdims=True)
    weights_low = (exponent / weight_sum).astype(BF)
    mixture = contract("hqk,khd->qhd", weights_low, value_rows)
    return (mixture.astype(BF), (row_max + jnp.log(weight_sum))[..., 0])


def attention_backward(queries, key_rows, value_rows, log_sums, grad_mix):
    score_scale = queries.shape[-1] ** (-0.5)
    scores = contract("qhd,khd->hqk", queries, key_rows) * score_scale
    weights_full = jnp.exp(scores - log_sums[..., None])
    grad_weights = contract("qhd,khd->hqk", grad_mix, value_rows)
    inner = jnp.sum(weights_full * grad_weights, -1, keepdims=True)
    grad_scores = (weights_full * (grad_weights - inner)).astype(BF)
    query_grad = contract("hqk,khd->qhd", grad_scores, key_rows) * score_scale
    key_grad = contract("hqk,qhd->khd", grad_scores, queries) * score_scale
    value_grad = contract("hqk,qhd->khd", weights_full.astype(BF), grad_mix)
    return (query_grad, key_grad, value_grad)


def on_device(
    tokens, skip_in, text_in, grid_pos, time_ids, cotangent,
    skip_weight, shift_weight, triple_weight, self_out_weight, cross_q_weight,
    cross_kv_weight, cross_out_weight, up_weight, down_weight,
    norm_gains, norm_biases, head_gains, head_biases, width_biases, column_biases, hidden_biases,
):
    batch, local_len, width = tokens.shape
    text_len = text_in.shape[1]
    head_size = head_gains.shape[1]
    z = lax.axis_index("shard")
    k = lax.axis_index("context")
    y = lax.axis_index("tensor")
    nz, nk, ny = lax.axis_size("shard"), lax.axis_size("context"), lax.axis_size("tensor")
    assert batch == ny == 2
    rows_z = triple_weight.shape[0]
    half_cols = triple_weight.shape[2]
    half_hidden = up_weight.shape[1]
    cb = half_cols // nk
    hb = half_hidden // nk
    eb = width // nk
    hh = cb // head_size
    heads = ny * hh
    length = local_len * nk
    sequences = batch * nz
    swap = [(0, 1), (1, 0)]

    def mine(values):
        return lax.dynamic_index_in_dim(values, y, 0, keepdims=False)

    def block(values, size, axis):
        return lax.dynamic_slice_in_dim(values, k * size, size, axis)

    def other(values):
        return lax.ppermute(values, "tensor", swap)

    pin = lax.optimization_barrier
    bits = [1 << i for i in range(nk.bit_length() - 1)]
    relative = jnp.arange(nk) ^ k

    def flip(values, axis_name, bit):
        count = lax.axis_size(axis_name)
        return lax.ppermute(values, axis_name, [(i, i ^ bit) for i in range(count)])

    def gather_far(values):
        for bit in reversed(bits[1:]):
            values = jnp.concatenate([values, flip(values, "context", bit)], 0)
        return values

    def gather_near(values):
        return jnp.concatenate([values, flip(values, "context", bits[0])], 0)

    def gather_rows(values):
        return gather_near(gather_far(values))

    order = [sum(((p >> j) & 1) << (len(bits) - 1 - j) for j in range(len(bits))) for p in range(nk)]

    def ranked(values, axis=0, back=False):
        where = (jnp.asarray(order) ^ k) if back else jnp.asarray(order)[relative]
        return jnp.take(values, where, axis=axis, indices_are_sorted=False, unique_indices=True)

    def partial_rows(pieces):
        half = pieces[0][0].shape[0] // 2

        def part(first):
            total = None
            for left, right, form in pieces:
                now = form(left[:half] if first else left[half:], right)
                total = now if total is None else total + now
            return total

        return part(False).astype(BF), part(True)

    def sum_rows(sent, total, fill=()):
        total = total + flip(sent, "context", bits[0]).astype(F32)
        for bit in bits[1:]:
            half = total.shape[0] // 2
            got = flip(total[half:].astype(BF), "context", bit)
            got, fill = pin((got, fill))
            total = total[:half] + got.astype(F32)
        return total, fill

    def scatter_rows(pieces):
        return sum_rows(*partial_rows(pieces))[0]

    def gather_filled(values, fill):
        for bit in reversed(bits[1:]):
            got = flip(values, "context", bit)
            got, fill = pin((got, fill))
            values = jnp.concatenate([values, got], 0)
        return gather_near(values), fill

    def by_batch(own, theirs):
        first = jnp.where(y == 0, own, theirs)
        second = jnp.where(y == 0, theirs, own)
        return jnp.stack([first, second])

    def gathered(values):
        return lax.all_gather(values, ("tensor", "shard"), axis=0, tiled=True)

    def halves(values):
        return (values[:width], values[width:])

    first_part = jnp.concatenate(
        [
            block(triple_weight, cb, 2).reshape(rows_z, 3 * cb),
            block(self_out_weight, cb, 0).T,
        ],
        1,
    )
    second_part = jnp.concatenate(
        [
            block(cross_q_weight, cb, 1),
            block(cross_kv_weight, cb, 2).reshape(rows_z, 2 * cb),
            block(cross_out_weight, cb, 0).T,
        ],
        1,
    )
    skip_part = jnp.pad(block(skip_weight, eb, 2).reshape(-1, eb), ((0, 0), (0, -eb % 128)))
    skip_z = lax.all_gather(skip_part, ("shard", "tensor"), axis=0, tiled=True)
    skip_block = jnp.transpose(skip_z[:, :eb].reshape(nz * ny, 2, -1, eb), (1, 0, 2, 3)).reshape(2 * width, eb)
    first_z = gathered(first_part)
    second_z = gathered(second_part)
    up_z = gathered(block(up_weight, hb, 1))
    down_z = gathered(block(down_weight, hb, 0).T)

    def own_columns(values, size, half):
        last = values.ndim - 1
        first = lax.dynamic_slice_in_dim(values, k * size, size, last)
        second = lax.dynamic_slice_in_dim(values, half + k * size, size, last)
        return (first, second)

    tok_rows, skip_rows, cot_rows = mine(tokens), mine(skip_in), mine(cotangent)
    text_rows = mine(text_in)
    grid_all = gather_rows(mine(grid_pos))
    cosine, sine_rows = rotary_tables(grid_all, head_size)
    times = lax.all_to_all(jnp.broadcast_to(time_ids, (nz, batch)), "shard", 0, 0, tiled=True).reshape(-1)
    silu_all = time_silu(times, width)
    shift_rows_count = shift_weight.shape[0]
    silu_rows = lax.dynamic_slice_in_dim(silu_all, (z * ny + y) * shift_rows_count, shift_rows_count, 1)
    shift_part = matmul(silu_rows, shift_weight).reshape(nz, ny, width)
    shift_mine = lax.dynamic_index_in_dim(shift_part, y, 1, keepdims=False)
    shift_give = lax.dynamic_index_in_dim(shift_part, 1 - y, 1, keepdims=False)
    shift_got = other(shift_give)
    shift_part = shift_mine + shift_got
    shift_row = jnp.sum(lax.all_to_all(shift_part, "shard", 0, 0, tiled=True), 0) + width_biases[1]

    tok_here = gather_far(jnp.concatenate([tok_rows, skip_rows], 1))
    tok_halves = (tok_here, flip(tok_here, "context", bits[0]))
    tok_halves, text_rows = pin((tok_halves, text_rows))
    summed_block = jnp.concatenate([matmul(t, skip_block).astype(BF) for t in tok_halves], 0)
    summed_block = ranked(summed_block.reshape(nk, local_len, eb)).reshape(length, eb)
    summed = lax.all_to_all(summed_block, "context", split_axis=0, concat_axis=1, tiled=True).astype(F32) + width_biases[0]

    first_pair = halves(first_z)
    triple_full = [w[:, : 3 * cb] for w in first_pair]
    self_out_full = [w[:, 3 * cb :] for w in first_pair]

    def first_piece(summed_in, shift_in, gain_rows, bias_rows):
        resid_out = layer_norm(summed_in, gain_rows[0], bias_rows[0])
        return (resid_out, layer_norm(resid_out, gain_rows[1], bias_rows[1]) + shift_in)

    (resid_zero, normed_one), pull_first = jax.vjp(first_piece, summed, shift_row, norm_gains, norm_biases)
    normed_one_all = gather_rows(normed_one.astype(BF))
    triple_bias = own_columns(column_biases[0:3], cb, half_cols)

    def to_heads(parts, count):
        return jnp.concatenate([p.reshape(p.shape[0], count, hh, head_size) for p in parts], 2)

    def from_heads(values):
        rows, count = values.shape[0], values.shape[1]
        return (values[:, :, :hh].reshape(rows, count * cb), values[:, :, hh:].reshape(rows, count * cb))

    triple = to_heads([matmul(normed_one_all, w) + b.reshape(1, -1) for w, b in zip(triple_full, triple_bias)], 3)

    def self_piece(triple_in, gain_rows, bias_rows):
        queries = rotate(layer_norm(triple_in[:, 0], gain_rows[0], bias_rows[0]), cosine, sine_rows)
        key_rows = rotate(layer_norm(triple_in[:, 1], gain_rows[1], bias_rows[1]), cosine, sine_rows)
        return (queries, key_rows, triple_in[:, 2])

    (query, key, value), pull_self = jax.vjp(self_piece, triple, head_gains, head_biases)
    query, key, value = query.astype(BF), key.astype(BF), value.astype(BF)
    query, key, value, cot_late = pin((query, key, value, cot_rows))
    cot_far = gather_far(cot_late)
    mix, self_sums = attention_forward(query, key, value)
    mix, cot_far = pin((mix, cot_far))
    mix_parts = from_heads(mix[:, None])
    resid_one = resid_zero + (
        scatter_rows([(mix_parts[0], self_out_full[0], contract_cols), (mix_parts[1], self_out_full[1], contract_cols)]) + width_biases[2]
    )


    resid_one, second_z = pin((resid_one, second_z))

    def second_piece(resid_in, gain_rows, bias_rows):
        return layer_norm(resid_in, gain_rows[2], bias_rows[2])

    normed_two, pull_second = jax.vjp(second_piece, resid_one, norm_gains, norm_biases)
    second_pair = halves(second_z)
    cross_q_full = [w[:, :cb] for w in second_pair]
    cross_kv_full = [w[:, cb : 3 * cb] for w in second_pair]
    cross_out_full = [w[:, 3 * cb :] for w in second_pair]
    normed_two_all = gather_rows(normed_two.astype(BF))
    cq_bias = own_columns(column_biases[3], cb, half_cols)
    kv_bias = own_columns(column_biases[4:6], cb, half_cols)
    cross_raw = to_heads([matmul(normed_two_all, w) + b.reshape(1, -1) for w, b in zip(cross_q_full, cq_bias)], 1)
    pair_raw = to_heads([matmul(text_rows, w) + b.reshape(1, -1) for w, b in zip(cross_kv_full, kv_bias)], 2)

    def cross_piece(query_in, pair_in, gain_rows, bias_rows):
        queries = rotate(layer_norm(query_in[:, 0], gain_rows[2], bias_rows[2]), cosine, sine_rows)
        key_rows = layer_norm(pair_in[:, 0], gain_rows[3], bias_rows[3])
        return (queries, key_rows, pair_in[:, 1])

    (cq, ck, cv), pull_cross = jax.vjp(cross_piece, cross_raw, pair_raw, head_gains, head_biases)
    cq, ck, cv = cq.astype(BF), ck.astype(BF), cv.astype(BF)
    cross_mix, cross_sums = attention_forward(cq, ck, cv)
    cross_parts = from_heads(cross_mix[:, None])
    resid_two = resid_one + (
        scatter_rows([(cross_parts[0], cross_out_full[0], contract_cols), (cross_parts[1], cross_out_full[1], contract_cols)]) + width_biases[3]
    )

    resid_two, up_z = pin((resid_two, up_z))

    def third_piece(resid_in, gain_rows, bias_rows):
        return layer_norm(resid_in, gain_rows[3], bias_rows[3])

    normed_three, pull_third = jax.vjp(third_piece, resid_two, norm_gains, norm_biases)
    normed_three_all = gather_rows(normed_three.astype(BF))
    up_full, down_full = halves(up_z), halves(down_z)
    normed_three_all, skip_late = pin((normed_three_all, skip_block))
    skip_far = gather_far(skip_late[None])
    hidden_bias = own_columns(hidden_biases, hb, half_hidden)

    def gelu_piece(hidden_in):
        return jax.nn.gelu(hidden_in, approximate=True)

    active, pull_gelu = [], []
    for w, b in zip(up_full, hidden_bias):
        act, pull = jax.vjp(gelu_piece, matmul(normed_three_all, w) + b)
        active.append(act.astype(BF))
        pull_gelu.append(pull)
    def stacked(parts):
        return jnp.concatenate([p.astype(BF) for p in parts], 0)

    def reduced(total):
        return lax.psum_scatter(total, ("tensor", "shard"), scatter_dimension=0, tiled=True)

    def own_first(parts):
        return (jnp.where(y == 0, parts[0], parts[1]), jnp.where(y == 0, parts[1], parts[0]))

    def over_shard(own, received):
        total = own + received.astype(F32)
        return lax.psum_scatter(total.astype(BF), "shard", scatter_dimension=0, tiled=True)

    def spread(values):
        values = values[None]
        for bit in reversed(bits):
            got, high = flip(values, "context", bit), (k & bit) != 0
            values = jnp.concatenate([jnp.where(high, got, values), jnp.where(high, values, got)], 0)
        return values

    def by_rank(values, count):
        depth = len(bits)
        rows = values.shape[1]
        values = values.reshape((2,) * depth + (rows, count, -1))
        back = tuple(reversed(range(depth)))
        return jnp.transpose(values, (depth, depth + 1) + back + (depth + 2,)).reshape(rows, count, -1)

    def columns_out(values, count):
        return by_rank(spread(values), count).astype(F32)

    def placed_out(got, size, first, count, form="prn,pnm->rm"):
        source = ((jnp.asarray(order) ^ k)[:, None] * size + jnp.arange(size)).astype(jnp.int32)
        select = (source[:, :, None] == jnp.arange(nk * size)).astype(BF)
        return [contract(form, got[:, :, i * size : (i + 1) * size], select) for i in range(first, first + count)]

    def rows_out(values):
        depth = len(bits)
        count, rows = values.shape[1:]
        values = values.reshape((2,) * depth + (count, rows))
        values = jnp.transpose(values, tuple(reversed(range(depth))) + (depth, depth + 1))
        return values.reshape(-1, rows).astype(F32)

    def wide_out(values):
        return jnp.concatenate([values[order[p]] for p in range(nk)], 1).astype(F32)

    cot_all = gather_near(cot_far)
    grad_out = cot_rows.astype(F32)
    down_sum = stacked([contract_rows(cot_all, a) for a in active])
    result_parts = partial_rows([(active[0], down_full[0], contract_cols), (active[1], down_full[1], contract_cols)])
    hidden_grad = [pull(matmul(cot_all, w))[0].astype(BF) for pull, w in zip(pull_gelu, down_full)]
    hidden_grad[0], hidden_grad[1], skip_far = pin((hidden_grad[0], hidden_grad[1], skip_far))
    skip_all = gather_near(skip_far)
    up_sum = stacked([contract_rows(normed_three_all, h) for h in hidden_grad])
    third_back = partial_rows([(hidden_grad[0], up_full[0], contract_cols), (hidden_grad[1], up_full[1], contract_cols)])
    third_back, result_parts = sum_rows(*third_back, result_parts)
    third_grads = pull_third(third_back)
    resid_two_grad = grad_out + third_grads[0]
    grad_two_low = resid_two_grad.astype(BF)
    grad_two_all = gather_rows(grad_two_low)
    down_grad = reduced(down_sum).T
    cross_out_grad = [contract_rows(grad_two_all, p).astype(BF) for p in cross_parts]
    cross_mix_grad = to_heads([matmul(grad_two_all, w).astype(BF) for w in cross_out_full], 1)[:, 0]
    cq_back, ck_back, cv_back = attention_backward(cq, ck, cv, cross_sums, cross_mix_grad)
    cross_grads = pull_cross((cq_back, ck_back, cv_back))
    cross_grad_low = from_heads(cross_grads[0].astype(BF))
    pair_low = from_heads(cross_grads[1].astype(BF))
    cross_q_grad = [contract_rows(normed_two_all, g).astype(BF) for g in cross_grad_low]
    cross_kv_grad = [contract_rows(text_rows, g).astype(BF) for g in pair_low]
    text_part = contract_cols(pair_low[0], cross_kv_full[0]) + contract_cols(pair_low[1], cross_kv_full[1])
    second_back = partial_rows(
        [(cross_grad_low[0], cross_q_full[0], contract_cols), (cross_grad_low[1], cross_q_full[1], contract_cols)]
    )
    second_back = sum_rows(*second_back)[0]
    text_part, up_grad = pin((text_part.astype(BF), reduced(up_sum)))
    text_part = lax.psum_scatter(text_part, "context", scatter_dimension=1, tiled=True)
    text_cols = text_part.shape[1] // ny
    second_grads = pull_second(second_back)
    resid_one_grad = resid_two_grad + second_grads[0]
    grad_one_low = resid_one_grad.astype(BF)
    grad_one_all, (cross_q_grad, cross_kv_grad, cross_out_grad) = gather_filled(
        grad_one_low, (cross_q_grad, cross_kv_grad, cross_out_grad)
    )
    self_out_grad = [contract_rows(grad_one_all, p).astype(BF) for p in mix_parts]
    small_grad = [jnp.concatenate(g, 1) for g in zip(cross_q_grad, cross_kv_grad, cross_out_grad, self_out_grad)]
    small_grad = own_first(small_grad)
    mix_grad = to_heads([matmul(grad_one_all, w).astype(BF) for w in self_out_full], 1)[:, 0]
    mix_grad, small_low, down_grad, result_parts = pin((mix_grad, small_grad[1], down_grad, result_parts))
    small_low = other(small_low)
    down_grad = spread(down_grad)
    result = resid_two + (sum_rows(*result_parts)[0] + width_biases[4])
    result_low = result.astype(BF)
    q_back, k_back, v_back = attention_backward(query, key, value, self_sums, mix_grad)
    q_back, k_back, v_back = q_back.astype(BF), k_back.astype(BF), v_back.astype(BF)
    self_grads = pull_self(
        (q_back.astype(F32), k_back.astype(F32), v_back.astype(F32))
    )
    triple_raw, small_low, up_grad = pin((self_grads[0].astype(BF), small_low, up_grad))
    small_grad = over_shard(small_grad[0].astype(F32), small_low)
    triple_low = from_heads(triple_raw)
    triple_grad = [contract_rows(normed_one_all, g) for g in own_first(triple_low)]
    triple_got = other(triple_grad[1].astype(BF))
    normed_grad = scatter_rows([(triple_low[0], triple_full[0], contract_cols), (triple_low[1], triple_full[1], contract_cols)])
    normed_grad, triple_got = pin((normed_grad, triple_got))
    first_grads = pull_first((resid_one_grad, normed_grad))
    summed_low = first_grads[0].astype(BF)
    triple_grad = over_shard(triple_grad[0], triple_got)
    summed_cols = lax.all_to_all(summed_low, "context", split_axis=1, concat_axis=0, tiled=True)
    summed_cols = ranked(summed_cols.reshape(nk, local_len, eb), 0, True).reshape(length, eb)
    skip_part = contract_rows(tok_halves[0], summed_cols[: length // 2]) + contract_rows(tok_halves[1], summed_cols[length // 2 :])
    skip_part, text_part, down_grad, result_low, up_grad, summed_late = pin(
        (skip_part.astype(BF), text_part, down_grad, result_low, up_grad, summed_low)
    )
    up_grad = spread(up_grad)
    text_mine = lax.dynamic_slice_in_dim(text_part, y * text_cols, text_cols, 1)
    skip_part = skip_part.reshape(2, nz, ny, -1, eb)
    keep = lax.dynamic_index_in_dim(skip_part, y, 2, keepdims=False)
    give = lax.dynamic_index_in_dim(skip_part, 1 - y, 2, keepdims=False)
    skip_total = (keep.astype(F32) + other(give).astype(F32)).astype(BF)
    skip_total, small_grad, triple_grad, result_low = pin((skip_total, small_grad, triple_grad, result_low))
    small_all = gather_rows(small_grad[None])
    result_out = by_batch(result_low, other(result_low)).astype(F32)
    text_theirs = other(lax.dynamic_slice_in_dim(text_part, (1 - y) * text_cols, text_cols, 1))
    text_grad = by_batch(text_mine, text_theirs).astype(F32)
    skip_total = jnp.transpose(skip_total, (1, 0, 2, 3)).reshape(-1, eb)

    both_low = by_batch(summed_late, other(summed_late)).reshape(batch * local_len, nk, eb)
    skip_grad = lax.psum_scatter(skip_total, "shard", scatter_dimension=0, tiled=True)
    triple_all = gather_rows(triple_grad[None])
    both_low = ranked(both_low, 1, True)
    tok_grad, skip_rows_grad = [
        contract("tke,kde->td", both_low, w).reshape(batch, local_len, width)
        for w in (skip_all[:, :width], skip_all[:, width:])
    ]

    triple_out = jnp.stack(placed_out(triple_all, cb, 0, 3), 1)
    small_out = (
        placed_out(small_all, cb, 4, 1, "prn,pnm->mr")[0],
        placed_out(small_all, cb, 0, 1)[0],
        jnp.stack(placed_out(small_all, cb, 1, 2), 1),
        placed_out(small_all, cb, 3, 1, "prn,pnm->mr")[0],
    )

    def place(parts, size, half, total):
        out = jnp.zeros(parts[0].shape[:-1] + (total,), F32)
        at = out.ndim - 1
        out = lax.dynamic_update_slice_in_dim(out, parts[0], k * size, at)
        return lax.dynamic_update_slice_in_dim(out, parts[1], half + k * size, at)

    def everywhere(parts, fills):
        flat = jnp.concatenate([p.reshape(-1) for p in parts])
        flat = pin((flat, skip_total))[0]
        size = flat.shape[0]
        flat = jnp.pad(flat, (0, -size % 1024)).reshape(-1, 128)
        stages = [(a, 1 << i) for a in ("context", "tensor", "shard") for i in range(lax.axis_size(a).bit_length() - 1)]
        fills = list(fills)
        for at, (axis_name, bit) in enumerate(stages):
            got = flip(flat, axis_name, bit)
            slot = at - len(stages) + len(fills)
            if slot >= 0:
                got, fills[slot] = pin((got, fills[slot]))
            flat = flat + got
        flat, out, at = flat.reshape(-1), [], 0
        for p in parts:
            out.append(flat[at : at + p.size].reshape(p.shape))
            at += p.size
        return out, fills

    def col_sums(values, count=1):
        return jnp.sum(values.astype(F32), 0).reshape(count, -1)

    gains_grad = first_grads[2] + second_grads[1] + third_grads[1]
    biases_grad = first_grads[3] + second_grads[2] + third_grads[2]
    head_gain_grad = self_grads[1] + cross_grads[2]
    head_bias_grad = self_grads[2] + cross_grads[3]
    width_grad = jnp.stack(
        [
            jnp.sum(summed_low.astype(F32), 0),
            first_grads[1],
            jnp.sum(grad_one_low.astype(F32), 0),
            jnp.sum(grad_two_low.astype(F32), 0),
            jnp.sum(grad_out, 0),
        ]
    )
    column_parts = [
        jnp.concatenate([col_sums(t, 3), col_sums(c, 1), col_sums(p, 2)], 0)
        for t, c, p in zip(triple_low, cross_grad_low, pair_low)
    ]
    column_grad = place(column_parts, cb, half_cols, width)
    hidden_grad_sum = place([col_sums(h)[0] for h in hidden_grad], hb, half_hidden, hidden_biases.shape[0])
    shift_slots = lax.dynamic_update_slice_in_dim(
        jnp.zeros((sequences, width), F32), first_grads[1][None], z * ny + y, 0
    )
    vectors, fills = everywhere(
        (gains_grad, biases_grad, head_gain_grad, head_bias_grad, width_grad, column_grad, hidden_grad_sum, shift_slots),
        (tok_grad, skip_rows_grad, (triple_out, small_out)),
    )
    tok_grad, skip_rows_grad, (triple_out, small_out) = fills
    skip_grad_out = placed_out(gather_rows(skip_grad[None]), eb, 0, 1)[0].reshape(2, -1, width)
    shift_grad_out = lax.dot_general(
        silu_rows.astype(F32), vectors[7], (((0,), (0,)), ((), ())), precision=lax.Precision.HIGHEST
    )

    return (
        result_out,
        tok_grad,
        skip_rows_grad,
        text_grad,
        skip_grad_out,
        shift_grad_out,
        triple_out,
        *small_out,
        wide_out(up_grad),
        rows_out(down_grad),
    ) + tuple(vectors[:7])


def solution(mesh):
    placed = (
        P("shard", "context", None),
        P("shard", "context", None),
        P("shard", None, None),
        P("shard", "context", None),
        P("shard"),
        P("shard", "context", None),
        P(None, ("shard", "tensor"), None),
        P(("shard", "tensor"), None),
        P("shard", None, "tensor"),
        P("tensor", "shard"),
        P("shard", "tensor"),
        P("shard", None, "tensor"),
        P("tensor", "shard"),
        P("shard", "tensor"),
        P("tensor", "shard"),
    ) + (P(),) * 7
    return jax.shard_map(
        on_device,
        mesh=mesh,
        in_specs=placed,
        out_specs=(
            P("shard", "context", None),
            P("shard", "context", None),
            P("shard", "context", None),
            P("shard", None, ("context", "tensor")),
        )
        + placed[6:15]
        + (P(),) * 7,
        check_vma=False,
    )
```

```python
import math

import jax
import jax.numpy as jnp
from jax import lax
from jax.sharding import PartitionSpec as P

epsilon = 1e-06
BF = jnp.bfloat16
F32 = jnp.float32


def matmul(left_side, right_side):
    return jnp.dot(left_side, right_side, preferred_element_type=F32)


def contract(form, left_side, right_side):
    return jnp.einsum(form, left_side, right_side, preferred_element_type=F32)


def contract_rows(left_side, right_side):
    return lax.dot_general(left_side, right_side, (((0,), (0,)), ((), ())), preferred_element_type=F32)


def contract_cols(left_side, right_side):
    return lax.dot_general(left_side, right_side, (((1,), (1,)), ((), ())), preferred_element_type=F32)


def layer_norm(values, scale_vec, offset):
    center = values - jnp.mean(values, -1, keepdims=True)
    spread = jnp.mean(center * center, -1, keepdims=True)
    return center * lax.rsqrt(spread + epsilon) * scale_vec + offset


def rotary_tables(grid_rows, head_size):
    quarter = head_size // 4
    frequencies = 1.0 / 10000.0 ** (jnp.arange(quarter, dtype=F32) * 2.0 / (head_size // 2))
    row_angle = grid_rows[:, 0:1].astype(F32) * frequencies
    col_angle = grid_rows[:, 1:2].astype(F32) * frequencies
    angles = jnp.concatenate([row_angle, row_angle, col_angle, col_angle], 1)
    return (jnp.cos(angles)[:, None, :], jnp.sin(angles)[:, None, :])


def rotate(values, cosine, sine_rows):
    quarter = values.shape[-1] // 4
    one = values[..., :quarter]
    two = values[..., quarter : 2 * quarter]
    three = values[..., 2 * quarter : 3 * quarter]
    four = values[..., 3 * quarter :]
    turned = jnp.concatenate([-two, one, -four, three], -1)
    return values * cosine + turned * sine_rows


def time_silu(stamps, model_width):
    half_width = model_width // 2
    frequencies = jnp.exp(-math.log(10000.0) * jnp.arange(half_width, dtype=F32) / half_width)
    angles = stamps.astype(F32)[:, None] * frequencies
    return jax.nn.silu(jnp.concatenate([jnp.cos(angles), jnp.sin(angles)], 1)).astype(BF)


def attention_forward(queries, key_rows, value_rows):
    score_scale = queries.shape[-1] ** (-0.5)
    scores = contract("qhd,khd->hqk", queries, key_rows) * score_scale
    row_max = jnp.max(scores, -1, keepdims=True)
    exponent = jnp.exp(scores - row_max)
    weight_sum = jnp.sum(exponent, -1, keepdims=True)
    weights_low = (exponent / weight_sum).astype(BF)
    mixture = contract("hqk,khd->qhd", weights_low, value_rows)
    return (mixture.astype(BF), (row_max + jnp.log(weight_sum))[..., 0])


def attention_backward(queries, key_rows, value_rows, log_sums, grad_mix):
    score_scale = queries.shape[-1] ** (-0.5)
    scores = contract("qhd,khd->hqk", queries, key_rows) * score_scale
    weights_full = jnp.exp(scores - log_sums[..., None])
    grad_weights = contract("qhd,khd->hqk", grad_mix, value_rows)
    inner = jnp.sum(weights_full * grad_weights, -1, keepdims=True)
    grad_scores = (weights_full * (grad_weights - inner)).astype(BF)
    query_grad = contract("hqk,khd->qhd", grad_scores, key_rows) * score_scale
    key_grad = contract("hqk,qhd->khd", grad_scores, queries) * score_scale
    value_grad = contract("hqk,qhd->khd", weights_full.astype(BF), grad_mix)
    return (query_grad, key_grad, value_grad)


def on_device(
    tokens, skip_in, text_in, grid_pos, time_ids, cotangent,
    skip_weight, shift_weight, triple_weight, self_out_weight, cross_q_weight,
    cross_kv_weight, cross_out_weight, up_weight, down_weight,
    norm_gains, norm_biases, head_gains, head_biases, width_biases, column_biases, hidden_biases,
):
    batch, local_len, width = tokens.shape
    text_len = text_in.shape[1]
    head_size = head_gains.shape[1]
    z = lax.axis_index("shard")
    k = lax.axis_index("context")
    y = lax.axis_index("tensor")
    nz, nk, ny = lax.axis_size("shard"), lax.axis_size("context"), lax.axis_size("tensor")
    assert batch == ny == 2
    rows_z = triple_weight.shape[0]
    half_cols = triple_weight.shape[2]
    half_hidden = up_weight.shape[1]
    cb = half_cols // nk
    hb = half_hidden // nk
    eb = width // nk
    hh = cb // head_size
    heads = ny * hh
    length = local_len * nk
    sequences = batch * nz
    swap = [(0, 1), (1, 0)]

    def mine(values):
        return lax.dynamic_index_in_dim(values, y, 0, keepdims=False)

    def block(values, size, axis):
        return lax.dynamic_slice_in_dim(values, k * size, size, axis)

    def other(values):
        return lax.ppermute(values, "tensor", swap)

    pin = lax.optimization_barrier
    bits = [1 << i for i in range(nk.bit_length() - 1)]
    relative = jnp.arange(nk) ^ k

    def flip(values, axis_name, bit):
        count = lax.axis_size(axis_name)
        return lax.ppermute(values, axis_name, [(i, i ^ bit) for i in range(count)])

    def gather_far(values):
        for bit in reversed(bits[1:]):
            values = jnp.concatenate([values, flip(values, "context", bit)], 0)
        return values

    def gather_near(values):
        return jnp.concatenate([values, flip(values, "context", bits[0])], 0)

    def gather_rows(values):
        blocks = [values]
        for bit in reversed(bits):
            blocks = blocks + [flip(b, "context", bit) for b in blocks]
        return jnp.concatenate(blocks, 0)

    order = [sum(((p >> j) & 1) << (len(bits) - 1 - j) for j in range(len(bits))) for p in range(nk)]

    def ranked(values, axis=0, back=False):
        where = (jnp.asarray(order) ^ k) if back else jnp.asarray(order)[relative]
        return jnp.take(values, where, axis=axis, indices_are_sorted=False, unique_indices=True)

    def partial_rows(pieces):
        half = pieces[0][0].shape[0] // 2

        def part(first):
            total = None
            for left, right, form in pieces:
                now = form(left[:half] if first else left[half:], right)
                total = now if total is None else total + now
            return total

        return part(False).astype(BF), part(True)

    def sum_rows(sent, total, fill=()):
        total = total + flip(sent, "context", bits[0]).astype(F32)
        for bit in bits[1:]:
            half = total.shape[0] // 2
            got = flip(total[half:].astype(BF), "context", bit)
            got, fill = pin((got, fill))
            total = total[:half] + got.astype(F32)
        return total, fill

    def scatter_rows(pieces):
        return sum_rows(*partial_rows(pieces))[0]

    def gather_filled(values, fill):
        blocks = [values]
        for bit in reversed(bits[1:]):
            got, fill = pin(([flip(b, "context", bit) for b in blocks], fill))
            blocks = blocks + got
        return jnp.concatenate(blocks + [flip(b, "context", bits[0]) for b in blocks], 0), fill

    def own_first(parts):
        return (jnp.where(y == 0, parts[0], parts[1]), jnp.where(y == 0, parts[1], parts[0]))

    def by_batch(own, theirs):
        first = jnp.where(y == 0, own, theirs)
        second = jnp.where(y == 0, theirs, own)
        return jnp.stack([first, second])

    def gathered(values):
        return lax.all_gather(values, ("tensor", "shard"), axis=0, tiled=True)

    def halves(values):
        return (values[:width], values[width:])

    first_part = jnp.concatenate(
        [
            block(triple_weight, cb, 2).reshape(rows_z, 3 * cb),
            block(self_out_weight, cb, 0).T,
        ],
        1,
    )
    second_part = jnp.concatenate(
        [
            block(cross_q_weight, cb, 1),
            block(cross_kv_weight, cb, 2).reshape(rows_z, 2 * cb),
            block(cross_out_weight, cb, 0).T,
        ],
        1,
    )
    skip_part = jnp.pad(block(skip_weight, eb, 2).reshape(-1, eb), ((0, 0), (0, -eb % 128)))
    skip_z = lax.all_gather(skip_part, ("shard", "tensor"), axis=0, tiled=True)
    skip_block = jnp.transpose(skip_z[:, :eb].reshape(nz * ny, 2, -1, eb), (1, 0, 2, 3)).reshape(2 * width, eb)
    first_z = gathered(first_part)
    second_z = lax.all_gather(second_part, "shard", axis=0, tiled=True)
    up_z = gathered(block(up_weight, hb, 1))
    down_z = gathered(block(down_weight, hb, 0).T)

    def own_columns(values, size, half):
        last = values.ndim - 1
        first = lax.dynamic_slice_in_dim(values, k * size, size, last)
        second = lax.dynamic_slice_in_dim(values, half + k * size, size, last)
        return (first, second)

    tok_rows, skip_rows, cot_rows = mine(tokens), mine(skip_in), mine(cotangent)
    text_rows = mine(text_in)
    grid_all = gather_rows(mine(grid_pos))
    cosine, sine_rows = rotary_tables(grid_all, head_size)
    times = lax.all_to_all(jnp.broadcast_to(time_ids, (nz, batch)), "shard", 0, 0, tiled=True).reshape(-1)
    silu_all = time_silu(times, width)
    shift_rows_count = shift_weight.shape[0]
    silu_rows = lax.dynamic_slice_in_dim(silu_all, (z * ny + y) * shift_rows_count, shift_rows_count, 1)
    shift_part = matmul(silu_rows, shift_weight).reshape(nz, ny, width)
    shift_mine = lax.dynamic_index_in_dim(shift_part, y, 1, keepdims=False)
    shift_give = lax.dynamic_index_in_dim(shift_part, 1 - y, 1, keepdims=False)
    shift_got = other(shift_give)
    shift_part = shift_mine + shift_got
    shift_row = jnp.sum(lax.all_to_all(shift_part, "shard", 0, 0, tiled=True), 0) + width_biases[1]

    tok_here = gather_far(jnp.concatenate([tok_rows, skip_rows], 1))
    tok_halves = (tok_here, flip(tok_here, "context", bits[0]))
    tok_halves, text_rows = pin((tok_halves, text_rows))
    summed_block = jnp.concatenate([matmul(t, skip_block).astype(BF) for t in tok_halves], 0)
    summed_block = ranked(summed_block.reshape(nk, local_len, eb)).reshape(length, eb)
    summed = lax.all_to_all(summed_block, "context", split_axis=0, concat_axis=1, tiled=True).astype(F32) + width_biases[0]

    first_pair = halves(first_z)
    triple_full = [w[:, : 3 * cb] for w in first_pair]
    self_out_full = [w[:, 3 * cb :] for w in first_pair]

    def first_piece(summed_in, shift_in, gain_rows, bias_rows):
        resid_out = layer_norm(summed_in, gain_rows[0], bias_rows[0])
        return (resid_out, layer_norm(resid_out, gain_rows[1], bias_rows[1]) + shift_in)

    (resid_zero, normed_one), pull_first = jax.vjp(first_piece, summed, shift_row, norm_gains, norm_biases)
    normed_one_all = gather_rows(normed_one.astype(BF))
    triple_bias = own_columns(column_biases[0:3], cb, half_cols)

    def to_heads(parts, count):
        return jnp.concatenate([p.reshape(p.shape[0], count, hh, head_size) for p in parts], 2)

    def from_heads(values):
        rows, count = values.shape[0], values.shape[1]
        return (values[:, :, :hh].reshape(rows, count * cb), values[:, :, hh:].reshape(rows, count * cb))

    triple = to_heads([matmul(normed_one_all, w) + b.reshape(1, -1) for w, b in zip(triple_full, triple_bias)], 3)

    def self_piece(triple_in, gain_rows, bias_rows):
        queries = rotate(layer_norm(triple_in[:, 0], gain_rows[0], bias_rows[0]), cosine, sine_rows)
        key_rows = rotate(layer_norm(triple_in[:, 1], gain_rows[1], bias_rows[1]), cosine, sine_rows)
        return (queries, key_rows, triple_in[:, 2])

    (query, key, value), pull_self = jax.vjp(self_piece, triple, head_gains, head_biases)
    query, key, value = query.astype(BF), key.astype(BF), value.astype(BF)
    query, key, value, cot_late = pin((query, key, value, cot_rows))
    cot_far = gather_far(cot_late)
    mix, self_sums = attention_forward(query, key, value)
    mix, cot_far = pin((mix, cot_far))
    mix_parts = from_heads(mix[:, None])
    resid_one = resid_zero + (
        scatter_rows([(mix_parts[0], self_out_full[0], contract_cols), (mix_parts[1], self_out_full[1], contract_cols)]) + width_biases[2]
    )


    resid_one, second_z, second_other = pin((resid_one, second_z, other(second_z)))

    def second_piece(resid_in, gain_rows, bias_rows):
        return layer_norm(resid_in, gain_rows[2], bias_rows[2])

    normed_two, pull_second = jax.vjp(second_piece, resid_one, norm_gains, norm_biases)
    second_pair = (second_z, second_other)
    cross_q_full = [w[:, :cb] for w in second_pair]
    cross_kv_full = [w[:, cb : 3 * cb] for w in second_pair]
    cross_out_full = [w[:, 3 * cb :] for w in second_pair]
    normed_two_all = gather_rows(normed_two.astype(BF))
    cq_bias = own_first(own_columns(column_biases[3], cb, half_cols))
    kv_bias = own_first(own_columns(column_biases[4:6], cb, half_cols))
    cross_raw = to_heads([matmul(normed_two_all, w) + b.reshape(1, -1) for w, b in zip(cross_q_full, cq_bias)], 1)
    pair_raw = to_heads([matmul(text_rows, w) + b.reshape(1, -1) for w, b in zip(cross_kv_full, kv_bias)], 2)

    def cross_piece(query_in, pair_in, gain_rows, bias_rows):
        queries = rotate(layer_norm(query_in[:, 0], gain_rows[2], bias_rows[2]), cosine, sine_rows)
        key_rows = layer_norm(pair_in[:, 0], gain_rows[3], bias_rows[3])
        return (queries, key_rows, pair_in[:, 1])

    (cq, ck, cv), pull_cross = jax.vjp(cross_piece, cross_raw, pair_raw, head_gains, head_biases)
    cq, ck, cv = cq.astype(BF), ck.astype(BF), cv.astype(BF)
    cross_mix, cross_sums = attention_forward(cq, ck, cv)
    cross_parts = from_heads(cross_mix[:, None])
    resid_two = resid_one + (
        scatter_rows([(cross_parts[0], cross_out_full[0], contract_cols), (cross_parts[1], cross_out_full[1], contract_cols)]) + width_biases[3]
    )

    resid_two, up_z = pin((resid_two, up_z))

    def third_piece(resid_in, gain_rows, bias_rows):
        return layer_norm(resid_in, gain_rows[3], bias_rows[3])

    normed_three, pull_third = jax.vjp(third_piece, resid_two, norm_gains, norm_biases)
    normed_three_all = gather_rows(normed_three.astype(BF))
    up_full, down_full = halves(up_z), halves(down_z)
    normed_three_all, skip_late = pin((normed_three_all, skip_block))
    skip_far = gather_far(skip_late[None])
    hidden_bias = own_columns(hidden_biases, hb, half_hidden)

    def gelu_piece(hidden_in):
        return jax.nn.gelu(hidden_in, approximate=True)

    active, pull_gelu = [], []
    for w, b in zip(up_full, hidden_bias):
        act, pull = jax.vjp(gelu_piece, matmul(normed_three_all, w) + b)
        active.append(act.astype(BF))
        pull_gelu.append(pull)
    def stacked(parts):
        return jnp.concatenate([p.astype(BF) for p in parts], 0)

    def reduced(total):
        return lax.psum_scatter(total, ("tensor", "shard"), scatter_dimension=0, tiled=True)

    def over_shard(own, received):
        total = own + received.astype(F32)
        return lax.psum_scatter(total.astype(BF), "shard", scatter_dimension=0, tiled=True)

    def spread(values):
        values = values[None]
        for bit in reversed(bits):
            got, high = flip(values, "context", bit), (k & bit) != 0
            values = jnp.concatenate([jnp.where(high, got, values), jnp.where(high, values, got)], 0)
        return values

    def by_rank(values, count):
        depth = len(bits)
        rows = values.shape[1]
        values = values.reshape((2,) * depth + (rows, count, -1))
        back = tuple(reversed(range(depth)))
        return jnp.transpose(values, (depth, depth + 1) + back + (depth + 2,)).reshape(rows, count, -1)

    def columns_out(values, count):
        return by_rank(spread(values), count).astype(F32)

    def placed_out(got, size, first, count, form="prn,pnm->rm"):
        source = ((jnp.asarray(order) ^ k)[:, None] * size + jnp.arange(size)).astype(jnp.int32)
        select = (source[:, :, None] == jnp.arange(nk * size)).astype(BF)
        return [contract(form, got[:, :, i * size : (i + 1) * size], select) for i in range(first, first + count)]

    def rows_out(values):
        depth = len(bits)
        count, rows = values.shape[1:]
        values = values.reshape((2,) * depth + (count, rows))
        values = jnp.transpose(values, tuple(reversed(range(depth))) + (depth, depth + 1))
        return values.reshape(-1, rows).astype(F32)

    def wide_out(values):
        return jnp.concatenate([values[order[p]] for p in range(nk)], 1).astype(F32)

    cot_all = gather_near(cot_far)
    grad_out = cot_rows.astype(F32)
    down_sum = stacked([contract_rows(cot_all, a) for a in active])
    result_parts = partial_rows([(active[0], down_full[0], contract_cols), (active[1], down_full[1], contract_cols)])
    hidden_grad = [pull(matmul(cot_all, w))[0].astype(BF) for pull, w in zip(pull_gelu, down_full)]
    hidden_grad[0], hidden_grad[1], skip_far = pin((hidden_grad[0], hidden_grad[1], skip_far))
    skip_all = gather_near(skip_far)
    up_sum = stacked([contract_rows(normed_three_all, h) for h in hidden_grad])
    third_back = partial_rows([(hidden_grad[0], up_full[0], contract_cols), (hidden_grad[1], up_full[1], contract_cols)])
    third_back, result_parts = sum_rows(*third_back, result_parts)
    third_grads = pull_third(third_back)
    resid_two_grad = grad_out + third_grads[0]
    grad_two_low = resid_two_grad.astype(BF)
    grad_two_all = gather_rows(grad_two_low)
    down_grad = reduced(down_sum).T
    cross_out_grad = [contract_rows(grad_two_all, p).astype(BF) for p in cross_parts]
    cross_mix_grad = to_heads([matmul(grad_two_all, w).astype(BF) for w in cross_out_full], 1)[:, 0]
    cq_back, ck_back, cv_back = attention_backward(cq, ck, cv, cross_sums, cross_mix_grad)
    cross_grads = pull_cross((cq_back, ck_back, cv_back))
    cross_grad_low = from_heads(cross_grads[0].astype(BF))
    pair_low = from_heads(cross_grads[1].astype(BF))
    cross_q_grad = [contract_rows(normed_two_all, g).astype(BF) for g in cross_grad_low]
    cross_kv_grad = [contract_rows(text_rows, g).astype(BF) for g in pair_low]
    text_part = contract_cols(pair_low[0], cross_kv_full[0]) + contract_cols(pair_low[1], cross_kv_full[1])
    second_back = partial_rows(
        [(cross_grad_low[0], cross_q_full[0], contract_cols), (cross_grad_low[1], cross_q_full[1], contract_cols)]
    )
    second_back = sum_rows(*second_back)[0]
    text_part, up_grad = pin((text_part.astype(BF), reduced(up_sum)))
    text_part = lax.psum_scatter(text_part, "context", scatter_dimension=1, tiled=True)
    text_cols = text_part.shape[1] // ny
    second_grads = pull_second(second_back)
    resid_one_grad = resid_two_grad + second_grads[0]
    grad_one_low = resid_one_grad.astype(BF)
    grad_one_all, (cross_q_grad, cross_kv_grad, cross_out_grad) = gather_filled(
        grad_one_low, (cross_q_grad, cross_kv_grad, cross_out_grad)
    )
    self_out_grad = [contract_rows(grad_one_all, p).astype(BF) for p in own_first(mix_parts)]
    small_grad = [jnp.concatenate(g, 1) for g in zip(cross_q_grad, cross_kv_grad, cross_out_grad, self_out_grad)]
    mix_grad = to_heads([matmul(grad_one_all, w).astype(BF) for w in self_out_full], 1)[:, 0]
    mix_grad, small_low, down_grad, result_parts = pin((mix_grad, small_grad[1], down_grad, result_parts))
    small_low = other(small_low)
    down_grad = spread(down_grad)
    result_part = result_parts[1] + flip(result_parts[0], "context", bits[0]).astype(F32)
    q_back, k_back, v_back = attention_backward(query, key, value, self_sums, mix_grad)
    q_back, k_back, v_back = q_back.astype(BF), k_back.astype(BF), v_back.astype(BF)
    self_grads = pull_self(
        (q_back.astype(F32), k_back.astype(F32), v_back.astype(F32))
    )
    triple_raw, small_low, up_grad = pin((self_grads[0].astype(BF), small_low, up_grad))
    small_total = (small_grad[0].astype(F32) + small_low.astype(F32)).astype(BF)
    small_grad = lax.psum_scatter(small_total, "shard", scatter_dimension=0, tiled=True)
    triple_low = from_heads(triple_raw)
    triple_grad = [contract_rows(normed_one_all, g) for g in own_first(triple_low)]
    triple_got = other(triple_grad[1].astype(BF))
    normed_grad = partial_rows([(triple_low[0], triple_full[0], contract_cols), (triple_low[1], triple_full[1], contract_cols)])
    normed_grad = sum_rows(*normed_grad, small_total[:8, :128])[0]
    normed_grad, triple_got = pin((normed_grad, triple_got))
    first_grads = pull_first((resid_one_grad, normed_grad))
    summed_low = first_grads[0].astype(BF)
    triple_grad = over_shard(triple_grad[0], triple_got)
    summed_cols = lax.all_to_all(summed_low, "context", split_axis=1, concat_axis=0, tiled=True)
    summed_cols = ranked(summed_cols.reshape(nk, local_len, eb), 0, True).reshape(length, eb)
    skip_part = contract_rows(tok_halves[0], summed_cols[: length // 2]) + contract_rows(tok_halves[1], summed_cols[length // 2 :])
    skip_part, text_part, down_grad, result_part, up_grad = pin(
        (skip_part.astype(BF), text_part, down_grad, result_part, up_grad)
    )
    for bit in bits[1:]:
        half = result_part.shape[0] // 2
        result_part = result_part[:half] + flip(result_part[half:].astype(BF), "context", bit).astype(F32)
    result_low = (resid_two + (result_part + width_biases[4])).astype(BF)
    up_grad = spread(up_grad)
    skip_part = skip_part.reshape(2, nz, ny, -1, eb)
    keep = lax.dynamic_index_in_dim(skip_part, y, 2, keepdims=False)
    give = lax.dynamic_index_in_dim(skip_part, 1 - y, 2, keepdims=False)
    skip_total = (keep.astype(F32) + other(give).astype(F32)).astype(BF)
    skip_total, small_grad, triple_grad, result_low, summed_late, text_part = pin(
        (skip_total, small_grad, triple_grad, result_low, summed_low, text_part)
    )
    text_mine = lax.dynamic_slice_in_dim(text_part, y * text_cols, text_cols, 1)
    text_theirs = other(lax.dynamic_slice_in_dim(text_part, (1 - y) * text_cols, text_cols, 1))
    text_grad = by_batch(text_mine, text_theirs).astype(F32)
    skip_total = jnp.transpose(skip_total, (1, 0, 2, 3)).reshape(-1, eb)

    both_low = by_batch(summed_late, other(summed_late)).reshape(batch * local_len, nk, eb)
    skip_grad = lax.psum_scatter(skip_total, "shard", scatter_dimension=0, tiled=True)
    both_low, skip_grad = pin((ranked(both_low, 1, True), skip_grad))
    tok_grad, skip_rows_grad = [
        contract("tke,kde->td", both_low, w).reshape(batch, local_len, width)
        for w in (skip_all[:, :width], skip_all[:, width:])
    ]

    def place(parts, size, half, total):
        out = jnp.zeros(parts[0].shape[:-1] + (total,), F32)
        at = out.ndim - 1
        out = lax.dynamic_update_slice_in_dim(out, parts[0], k * size, at)
        return lax.dynamic_update_slice_in_dim(out, parts[1], half + k * size, at)

    def flattened(parts):
        flat = jnp.concatenate([p.reshape(-1) for p in parts])
        return jnp.pad(flat, (0, -flat.shape[0] % 1024)).reshape(-1, 128)

    def restored(flat, parts):
        flat, out, at = flat.reshape(-1), [], 0
        for p in parts:
            out.append(flat[at : at + p.size].reshape(p.shape))
            at += p.size
        return out

    def summed_over(flat, axis_name, bit, fill):
        got, fill = pin((flip(flat, axis_name, bit), fill))
        return flat + got, fill

    def col_sums(values, count=1):
        return jnp.sum(values.astype(F32), 0).reshape(count, -1)

    gains_grad = first_grads[2] + second_grads[1] + third_grads[1]
    biases_grad = first_grads[3] + second_grads[2] + third_grads[2]
    head_gain_grad = self_grads[1] + cross_grads[2]
    head_bias_grad = self_grads[2] + cross_grads[3]
    width_grad = jnp.stack(
        [
            jnp.sum(summed_low.astype(F32), 0),
            first_grads[1],
            jnp.sum(grad_one_low.astype(F32), 0),
            jnp.sum(grad_two_low.astype(F32), 0),
            jnp.sum(grad_out, 0),
        ]
    )
    column_parts = [
        jnp.concatenate([t, c], 0)
        for t, c in zip(
            [col_sums(t, 3) for t in triple_low],
            own_first([jnp.concatenate([col_sums(c, 1), col_sums(p, 2)], 0) for c, p in zip(cross_grad_low, pair_low)]),
        )
    ]
    column_grad = place(column_parts, cb, half_cols, width)
    hidden_grad_sum = place([col_sums(h)[0] for h in hidden_grad], hb, half_hidden, hidden_biases.shape[0])
    shift_slots = lax.dynamic_update_slice_in_dim(
        jnp.zeros((sequences, width), F32), first_grads[1][None], z * ny + y, 0
    )
    parts = (gains_grad, biases_grad, head_gain_grad, head_bias_grad, width_grad, column_grad, hidden_grad_sum, shift_slots)
    flat, skip_total = pin((flattened(parts), skip_total))
    for bit in bits:
        flat, (small_grad, triple_grad) = summed_over(flat, "context", bit, (small_grad, triple_grad))
    small_all, triple_all = gather_rows(small_grad[None]), gather_rows(triple_grad[None])
    triple_out = jnp.stack(placed_out(triple_all, cb, 0, 3), 1)
    small_out = (
        placed_out(small_all, cb, 4, 1, "prn,pnm->mr")[0],
        placed_out(small_all, cb, 0, 1)[0],
        jnp.stack(placed_out(small_all, cb, 1, 2), 1),
        placed_out(small_all, cb, 3, 1, "prn,pnm->mr")[0],
    )

    for i in range(ny.bit_length() - 1):
        flat, (tok_grad, result_low) = summed_over(flat, "tensor", 1 << i, (tok_grad, result_low))
    result_out = by_batch(result_low, other(result_low)).astype(F32)
    skip_gathered = gather_rows(skip_grad[None])
    for i in range(nz.bit_length() - 1):
        if i == 0:
            flat, (skip_rows_grad, skip_gathered) = summed_over(flat, "shard", 1, (skip_rows_grad, skip_gathered))
        else:
            flat, (triple_out, small_out) = summed_over(flat, "shard", 1 << i, (triple_out, small_out))
    vectors = restored(flat, parts)
    skip_grad_out = placed_out(skip_gathered, eb, 0, 1)[0].reshape(2, -1, width)
    shift_grad_out = lax.dot_general(
        silu_rows.astype(F32), vectors[7], (((0,), (0,)), ((), ())), precision=lax.Precision.HIGHEST
    )

    return (
        result_out,
        tok_grad,
        skip_rows_grad,
        text_grad,
        skip_grad_out,
        shift_grad_out,
        triple_out,
        *small_out,
        wide_out(up_grad),
        rows_out(down_grad),
    ) + tuple(vectors[:7])


def solution(mesh):
    placed = (
        P("shard", "context", None),
        P("shard", "context", None),
        P("shard", None, None),
        P("shard", "context", None),
        P("shard"),
        P("shard", "context", None),
        P(None, ("shard", "tensor"), None),
        P(("shard", "tensor"), None),
        P("shard", None, "tensor"),
        P("tensor", "shard"),
        P("shard", "tensor"),
        P("shard", None, "tensor"),
        P("tensor", "shard"),
        P("shard", "tensor"),
        P("tensor", "shard"),
    ) + (P(),) * 7
    return jax.shard_map(
        on_device,
        mesh=mesh,
        in_specs=placed,
        out_specs=(
            P("shard", "context", None),
            P("shard", "context", None),
            P("shard", "context", None),
            P("shard", None, ("context", "tensor")),
        )
        + placed[6:15]
        + (P(),) * 7,
        check_vma=False,
    )
```

```python
import math

import jax
import jax.numpy as jnp
from jax import lax
from jax.sharding import PartitionSpec as P

epsilon = 1e-06
BF = jnp.bfloat16
F32 = jnp.float32


def matmul(left_side, right_side):
    return jnp.dot(left_side, right_side, preferred_element_type=F32)


def contract(form, left_side, right_side):
    return jnp.einsum(form, left_side, right_side, preferred_element_type=F32)


def contract_rows(left_side, right_side):
    return lax.dot_general(left_side, right_side, (((0,), (0,)), ((), ())), preferred_element_type=F32)


def contract_cols(left_side, right_side):
    return lax.dot_general(left_side, right_side, (((1,), (1,)), ((), ())), preferred_element_type=F32)


def layer_norm(values, scale_vec, offset):
    center = values - jnp.mean(values, -1, keepdims=True)
    spread = jnp.mean(center * center, -1, keepdims=True)
    return center * lax.rsqrt(spread + epsilon) * scale_vec + offset


def rotary_tables(grid_rows, head_size):
    quarter = head_size // 4
    frequencies = 1.0 / 10000.0 ** (jnp.arange(quarter, dtype=F32) * 2.0 / (head_size // 2))
    row_angle = grid_rows[:, 0:1].astype(F32) * frequencies
    col_angle = grid_rows[:, 1:2].astype(F32) * frequencies
    angles = jnp.concatenate([row_angle, row_angle, col_angle, col_angle], 1)
    return (jnp.cos(angles)[:, None, :], jnp.sin(angles)[:, None, :])


def rotate(values, cosine, sine_rows):
    quarter = values.shape[-1] // 4
    one = values[..., :quarter]
    two = values[..., quarter : 2 * quarter]
    three = values[..., 2 * quarter : 3 * quarter]
    four = values[..., 3 * quarter :]
    turned = jnp.concatenate([-two, one, -four, three], -1)
    return values * cosine + turned * sine_rows


def time_silu(stamps, model_width):
    half_width = model_width // 2
    frequencies = jnp.exp(-math.log(10000.0) * jnp.arange(half_width, dtype=F32) / half_width)
    angles = stamps.astype(F32)[:, None] * frequencies
    return jax.nn.silu(jnp.concatenate([jnp.cos(angles), jnp.sin(angles)], 1)).astype(BF)


def attention_forward(queries, key_rows, value_rows):
    score_scale = queries.shape[-1] ** (-0.5)
    scores = contract("qhd,khd->hqk", queries, key_rows) * score_scale
    row_max = jnp.max(scores, -1, keepdims=True)
    exponent = jnp.exp(scores - row_max)
    weight_sum = jnp.sum(exponent, -1, keepdims=True)
    weights_low = (exponent / weight_sum).astype(BF)
    mixture = contract("hqk,khd->qhd", weights_low, value_rows)
    return (mixture.astype(BF), (row_max + jnp.log(weight_sum))[..., 0])


def attention_backward(queries, key_rows, value_rows, log_sums, grad_mix):
    score_scale = queries.shape[-1] ** (-0.5)
    scores = contract("qhd,khd->hqk", queries, key_rows) * score_scale
    weights_full = jnp.exp(scores - log_sums[..., None])
    grad_weights = contract("qhd,khd->hqk", grad_mix, value_rows)
    inner = jnp.sum(weights_full * grad_weights, -1, keepdims=True)
    grad_scores = (weights_full * (grad_weights - inner)).astype(BF)
    query_grad = contract("hqk,khd->qhd", grad_scores, key_rows) * score_scale
    key_grad = contract("hqk,qhd->khd", grad_scores, queries) * score_scale
    value_grad = contract("hqk,qhd->khd", weights_full.astype(BF), grad_mix)
    return (query_grad, key_grad, value_grad)


def on_device(
    tokens, skip_in, text_in, grid_pos, time_ids, cotangent,
    skip_weight, shift_weight, triple_weight, self_out_weight, cross_q_weight,
    cross_kv_weight, cross_out_weight, up_weight, down_weight,
    norm_gains, norm_biases, head_gains, head_biases, width_biases, column_biases, hidden_biases,
):
    batch, local_len, width = tokens.shape
    text_len = text_in.shape[1]
    head_size = head_gains.shape[1]
    z = lax.axis_index("shard")
    k = lax.axis_index("context")
    y = lax.axis_index("tensor")
    nz, nk, ny = lax.axis_size("shard"), lax.axis_size("context"), lax.axis_size("tensor")
    assert batch == ny == 2
    rows_z = triple_weight.shape[0]
    half_cols = triple_weight.shape[2]
    half_hidden = up_weight.shape[1]
    cb = half_cols // nk
    hb = half_hidden // nk
    eb = width // nk
    hh = cb // head_size
    heads = ny * hh
    length = local_len * nk
    sequences = batch * nz
    swap = [(0, 1), (1, 0)]

    def mine(values):
        return lax.dynamic_index_in_dim(values, y, 0, keepdims=False)

    def block(values, size, axis):
        return lax.dynamic_slice_in_dim(values, k * size, size, axis)

    def other(values):
        return lax.ppermute(values, "tensor", swap)

    pin = lax.optimization_barrier
    bits = [1 << i for i in range(nk.bit_length() - 1)]
    relative = jnp.arange(nk) ^ k

    def flip(values, axis_name, bit):
        count = lax.axis_size(axis_name)
        return lax.ppermute(values, axis_name, [(i, i ^ bit) for i in range(count)])

    def gather_far(values):
        for bit in reversed(bits[1:]):
            values = jnp.concatenate([values, flip(values, "context", bit)], 0)
        return values

    def gather_near(values):
        return jnp.concatenate([values, flip(values, "context", bits[0])], 0)

    def gather_rows(values):
        blocks = [values]
        for bit in reversed(bits):
            blocks = blocks + [flip(b, "context", bit) for b in blocks]
        return jnp.concatenate(blocks, 0)

    order = [sum(((p >> j) & 1) << (len(bits) - 1 - j) for j in range(len(bits))) for p in range(nk)]

    def ranked(values, axis=0, back=False):
        where = (jnp.asarray(order) ^ k) if back else jnp.asarray(order)[relative]
        return jnp.take(values, where, axis=axis, indices_are_sorted=False, unique_indices=True)

    def partial_rows(pieces):
        half = pieces[0][0].shape[0] // 2

        def part(first):
            total = None
            for left, right, form in pieces:
                now = form(left[:half] if first else left[half:], right)
                total = now if total is None else total + now
            return total

        return part(False).astype(BF), part(True)

    def sum_rows(sent, total, fill=()):
        total = total + flip(sent, "context", bits[0]).astype(F32)
        for bit in bits[1:]:
            half = total.shape[0] // 2
            got = flip(total[half:].astype(BF), "context", bit)
            got, fill = pin((got, fill))
            total = total[:half] + got.astype(F32)
        return total, fill

    def scatter_rows(pieces):
        return sum_rows(*partial_rows(pieces))[0]

    def gather_filled(values, fill):
        blocks = [values]
        for bit in reversed(bits[1:]):
            got, fill = pin(([flip(b, "context", bit) for b in blocks], fill))
            blocks = blocks + got
        return jnp.concatenate(blocks + [flip(b, "context", bits[0]) for b in blocks], 0), fill

    def own_first(parts):
        return (jnp.where(y == 0, parts[0], parts[1]), jnp.where(y == 0, parts[1], parts[0]))

    def by_batch(own, theirs):
        first = jnp.where(y == 0, own, theirs)
        second = jnp.where(y == 0, theirs, own)
        return jnp.stack([first, second])

    def gathered(values):
        return lax.all_gather(values, ("tensor", "shard"), axis=0, tiled=True)

    def halves(values):
        return (values[:width], values[width:])

    first_part = jnp.concatenate(
        [
            block(triple_weight, cb, 2).reshape(rows_z, 3 * cb),
            block(self_out_weight, cb, 0).T,
        ],
        1,
    )
    second_part = jnp.concatenate(
        [
            block(cross_q_weight, cb, 1),
            block(cross_kv_weight, cb, 2).reshape(rows_z, 2 * cb),
            block(cross_out_weight, cb, 0).T,
        ],
        1,
    )
    skip_part = jnp.pad(block(skip_weight, eb, 2).reshape(-1, eb), ((0, 0), (0, -eb % 128)))
    skip_z = lax.all_gather(skip_part, ("shard", "tensor"), axis=0, tiled=True)
    skip_block = jnp.transpose(skip_z[:, :eb].reshape(nz * ny, 2, -1, eb), (1, 0, 2, 3)).reshape(2 * width, eb)
    first_z = gathered(first_part)
    second_z = lax.all_gather(second_part, "shard", axis=0, tiled=True)
    up_z = gathered(block(up_weight, hb, 1))
    down_z = gathered(block(down_weight, hb, 0).T)

    def own_columns(values, size, half):
        last = values.ndim - 1
        first = lax.dynamic_slice_in_dim(values, k * size, size, last)
        second = lax.dynamic_slice_in_dim(values, half + k * size, size, last)
        return (first, second)

    tok_rows, skip_rows, cot_rows = mine(tokens), mine(skip_in), mine(cotangent)
    text_rows = mine(text_in)
    grid_all = gather_rows(mine(grid_pos))
    cosine, sine_rows = rotary_tables(grid_all, head_size)
    times = lax.all_to_all(jnp.broadcast_to(time_ids, (nz, batch)), "shard", 0, 0, tiled=True).reshape(-1)
    silu_all = time_silu(times, width)
    shift_rows_count = shift_weight.shape[0]
    silu_rows = lax.dynamic_slice_in_dim(silu_all, (z * ny + y) * shift_rows_count, shift_rows_count, 1)
    shift_part = matmul(silu_rows, shift_weight).reshape(nz, ny, width)
    shift_mine = lax.dynamic_index_in_dim(shift_part, y, 1, keepdims=False)
    shift_give = lax.dynamic_index_in_dim(shift_part, 1 - y, 1, keepdims=False)
    shift_got = other(shift_give)
    shift_part = shift_mine + shift_got
    shift_row = jnp.sum(lax.all_to_all(shift_part, "shard", 0, 0, tiled=True), 0) + width_biases[1]

    tok_here = gather_far(jnp.concatenate([tok_rows, skip_rows], 1))
    tok_halves = (tok_here, flip(tok_here, "context", bits[0]))
    tok_halves, text_rows = pin((tok_halves, text_rows))
    summed_block = jnp.concatenate([matmul(t, skip_block).astype(BF) for t in tok_halves], 0)
    summed_block = ranked(summed_block.reshape(nk, local_len, eb)).reshape(length, eb)
    summed = lax.all_to_all(summed_block, "context", split_axis=0, concat_axis=1, tiled=True).astype(F32) + width_biases[0]

    first_pair = halves(first_z)
    triple_full = [w[:, : 3 * cb] for w in first_pair]
    self_out_full = [w[:, 3 * cb :] for w in first_pair]

    def first_piece(summed_in, shift_in, gain_rows, bias_rows):
        resid_out = layer_norm(summed_in, gain_rows[0], bias_rows[0])
        return (resid_out, layer_norm(resid_out, gain_rows[1], bias_rows[1]) + shift_in)

    (resid_zero, normed_one), pull_first = jax.vjp(first_piece, summed, shift_row, norm_gains, norm_biases)
    normed_one_all = gather_rows(normed_one.astype(BF))
    triple_bias = own_columns(column_biases[0:3], cb, half_cols)

    def to_heads(parts, count):
        return jnp.concatenate([p.reshape(p.shape[0], count, hh, head_size) for p in parts], 2)

    def from_heads(values):
        rows, count = values.shape[0], values.shape[1]
        return (values[:, :, :hh].reshape(rows, count * cb), values[:, :, hh:].reshape(rows, count * cb))

    triple = to_heads([matmul(normed_one_all, w) + b.reshape(1, -1) for w, b in zip(triple_full, triple_bias)], 3)

    def self_piece(triple_in, gain_rows, bias_rows):
        queries = rotate(layer_norm(triple_in[:, 0], gain_rows[0], bias_rows[0]), cosine, sine_rows)
        key_rows = rotate(layer_norm(triple_in[:, 1], gain_rows[1], bias_rows[1]), cosine, sine_rows)
        return (queries, key_rows, triple_in[:, 2])

    (query, key, value), pull_self = jax.vjp(self_piece, triple, head_gains, head_biases)
    query, key, value = query.astype(BF), key.astype(BF), value.astype(BF)
    query, key, value, cot_late = pin((query, key, value, cot_rows))
    cot_far = gather_far(cot_late)
    mix, self_sums = attention_forward(query, key, value)
    mix, cot_far = pin((mix, cot_far))
    mix_parts = from_heads(mix[:, None])
    resid_one = resid_zero + (
        scatter_rows([(mix_parts[0], self_out_full[0], contract_cols), (mix_parts[1], self_out_full[1], contract_cols)]) + width_biases[2]
    )


    resid_one, second_z, second_other = pin((resid_one, second_z, other(second_z)))

    def second_piece(resid_in, gain_rows, bias_rows):
        return layer_norm(resid_in, gain_rows[2], bias_rows[2])

    normed_two, pull_second = jax.vjp(second_piece, resid_one, norm_gains, norm_biases)
    second_pair = (second_z, second_other)
    cross_q_full = [w[:, :cb] for w in second_pair]
    cross_kv_full = [w[:, cb : 3 * cb] for w in second_pair]
    cross_out_full = [w[:, 3 * cb :] for w in second_pair]
    normed_two_all = gather_rows(normed_two.astype(BF))
    cq_bias = own_first(own_columns(column_biases[3], cb, half_cols))
    kv_bias = own_first(own_columns(column_biases[4:6], cb, half_cols))
    cross_raw = to_heads([matmul(normed_two_all, w) + b.reshape(1, -1) for w, b in zip(cross_q_full, cq_bias)], 1)
    pair_raw = to_heads([matmul(text_rows, w) + b.reshape(1, -1) for w, b in zip(cross_kv_full, kv_bias)], 2)

    def cross_piece(query_in, pair_in, gain_rows, bias_rows):
        queries = rotate(layer_norm(query_in[:, 0], gain_rows[2], bias_rows[2]), cosine, sine_rows)
        key_rows = layer_norm(pair_in[:, 0], gain_rows[3], bias_rows[3])
        return (queries, key_rows, pair_in[:, 1])

    (cq, ck, cv), pull_cross = jax.vjp(cross_piece, cross_raw, pair_raw, head_gains, head_biases)
    cq, ck, cv = cq.astype(BF), ck.astype(BF), cv.astype(BF)
    cross_mix, cross_sums = attention_forward(cq, ck, cv)
    cross_parts = from_heads(cross_mix[:, None])
    resid_two = resid_one + (
        scatter_rows([(cross_parts[0], cross_out_full[0], contract_cols), (cross_parts[1], cross_out_full[1], contract_cols)]) + width_biases[3]
    )

    resid_two, up_z = pin((resid_two, up_z))

    def third_piece(resid_in, gain_rows, bias_rows):
        return layer_norm(resid_in, gain_rows[3], bias_rows[3])

    normed_three, pull_third = jax.vjp(third_piece, resid_two, norm_gains, norm_biases)
    normed_three_all = gather_rows(normed_three.astype(BF))
    up_full, down_full = halves(up_z), halves(down_z)
    normed_three_all, skip_late = pin((normed_three_all, skip_block))
    skip_far = gather_far(skip_late[None])
    hidden_bias = own_columns(hidden_biases, hb, half_hidden)

    def gelu_piece(hidden_in):
        return jax.nn.gelu(hidden_in, approximate=True)

    active, pull_gelu = [], []
    for w, b in zip(up_full, hidden_bias):
        act, pull = jax.vjp(gelu_piece, matmul(normed_three_all, w) + b)
        active.append(act.astype(BF))
        pull_gelu.append(pull)
    def stacked(parts):
        return jnp.concatenate([p.astype(BF) for p in parts], 0)

    def reduced(total):
        return lax.psum_scatter(total, ("tensor", "shard"), scatter_dimension=0, tiled=True)

    def over_shard(own, received):
        total = own + received.astype(F32)
        return lax.psum_scatter(total.astype(BF), "shard", scatter_dimension=0, tiled=True)

    def spread(values):
        values = values[None]
        for bit in reversed(bits):
            got, high = flip(values, "context", bit), (k & bit) != 0
            values = jnp.concatenate([jnp.where(high, got, values), jnp.where(high, values, got)], 0)
        return values

    def by_rank(values, count):
        depth = len(bits)
        rows = values.shape[1]
        values = values.reshape((2,) * depth + (rows, count, -1))
        back = tuple(reversed(range(depth)))
        return jnp.transpose(values, (depth, depth + 1) + back + (depth + 2,)).reshape(rows, count, -1)

    def columns_out(values, count):
        return by_rank(spread(values), count).astype(F32)

    def placed_out(got, size, first, count, form="prn,pnm->rm"):
        source = ((jnp.asarray(order) ^ k)[:, None] * size + jnp.arange(size)).astype(jnp.int32)
        select = (source[:, :, None] == jnp.arange(nk * size)).astype(BF)
        return [contract(form, got[:, :, i * size : (i + 1) * size], select) for i in range(first, first + count)]

    def rows_out(values):
        depth = len(bits)
        count, rows = values.shape[1:]
        values = values.reshape((2,) * depth + (count, rows))
        values = jnp.transpose(values, tuple(reversed(range(depth))) + (depth, depth + 1))
        return values.reshape(-1, rows).astype(F32)

    def wide_out(values):
        return jnp.concatenate([values[order[p]] for p in range(nk)], 1).astype(F32)

    cot_all = gather_near(cot_far)
    grad_out = cot_rows.astype(F32)
    down_sum = stacked([contract_rows(cot_all, a) for a in active])
    result_parts = partial_rows([(active[0], down_full[0], contract_cols), (active[1], down_full[1], contract_cols)])
    hidden_grad = [pull(matmul(cot_all, w))[0].astype(BF) for pull, w in zip(pull_gelu, down_full)]
    hidden_grad[0], hidden_grad[1], skip_far = pin((hidden_grad[0], hidden_grad[1], skip_far))
    skip_all = gather_near(skip_far)
    up_sum = stacked([contract_rows(normed_three_all, h) for h in hidden_grad])
    third_back = partial_rows([(hidden_grad[0], up_full[0], contract_cols), (hidden_grad[1], up_full[1], contract_cols)])
    third_back, result_parts = sum_rows(*third_back, result_parts)
    third_grads = pull_third(third_back)
    resid_two_grad = grad_out + third_grads[0]
    grad_two_low = resid_two_grad.astype(BF)
    grad_two_all = gather_rows(grad_two_low)
    down_grad = reduced(down_sum)
    cross_out_grad = [contract_rows(grad_two_all, p).astype(BF) for p in cross_parts]
    cross_mix_grad = to_heads([matmul(grad_two_all, w).astype(BF) for w in cross_out_full], 1)[:, 0]
    cq_back, ck_back, cv_back = attention_backward(cq, ck, cv, cross_sums, cross_mix_grad)
    cross_grads = pull_cross((cq_back, ck_back, cv_back))
    cross_grad_low = from_heads(cross_grads[0].astype(BF))
    pair_low = from_heads(cross_grads[1].astype(BF))
    cross_q_grad = [contract_rows(normed_two_all, g).astype(BF) for g in cross_grad_low]
    cross_kv_grad = [contract_rows(text_rows, g).astype(BF) for g in pair_low]
    text_part = contract_cols(pair_low[0], cross_kv_full[0]) + contract_cols(pair_low[1], cross_kv_full[1])
    second_back = partial_rows(
        [(cross_grad_low[0], cross_q_full[0], contract_cols), (cross_grad_low[1], cross_q_full[1], contract_cols)]
    )
    second_back = sum_rows(*second_back)[0]
    text_part, up_grad = pin((text_part.astype(BF), reduced(up_sum)))
    text_part = lax.psum_scatter(text_part, "context", scatter_dimension=1, tiled=True)
    text_cols = text_part.shape[1] // ny
    second_grads = pull_second(second_back)
    resid_one_grad = resid_two_grad + second_grads[0]
    grad_one_low = resid_one_grad.astype(BF)
    grad_one_all, (cross_q_grad, cross_kv_grad, cross_out_grad) = gather_filled(
        grad_one_low, (cross_q_grad, cross_kv_grad, cross_out_grad)
    )
    self_out_grad = [contract_rows(grad_one_all, p).astype(BF) for p in own_first(mix_parts)]
    small_grad = [jnp.concatenate(g, 1) for g in zip(cross_q_grad, cross_kv_grad, cross_out_grad, self_out_grad)]
    mix_grad = to_heads([matmul(grad_one_all, w).astype(BF) for w in self_out_full], 1)[:, 0]
    mix_grad, small_low, down_grad, result_parts = pin((mix_grad, small_grad[1], down_grad, result_parts))
    small_low = other(small_low)
    down_grad = spread(down_grad)
    result_part = result_parts[1] + flip(result_parts[0], "context", bits[0]).astype(F32)
    q_back, k_back, v_back = attention_backward(query, key, value, self_sums, mix_grad)
    q_back, k_back, v_back = q_back.astype(BF), k_back.astype(BF), v_back.astype(BF)
    self_grads = pull_self(
        (q_back.astype(F32), k_back.astype(F32), v_back.astype(F32))
    )
    triple_raw, small_low, up_grad = pin((self_grads[0].astype(BF), small_low, up_grad))
    small_total = (small_grad[0].astype(F32) + small_low.astype(F32)).astype(BF)
    small_grad = lax.psum_scatter(small_total, "shard", scatter_dimension=0, tiled=True)
    triple_low = from_heads(triple_raw)
    triple_grad = [contract_rows(normed_one_all, g) for g in own_first(triple_low)]
    triple_got = other(triple_grad[1].astype(BF))
    normed_grad = partial_rows([(triple_low[0], triple_full[0], contract_cols), (triple_low[1], triple_full[1], contract_cols)])
    normed_grad = sum_rows(*normed_grad, small_total[:8, :128])[0]
    normed_grad, triple_got = pin((normed_grad, triple_got))
    first_grads = pull_first((resid_one_grad, normed_grad))
    summed_low = first_grads[0].astype(BF)
    triple_grad = over_shard(triple_grad[0], triple_got)
    summed_cols = lax.all_to_all(summed_low, "context", split_axis=1, concat_axis=0, tiled=True)
    summed_cols = ranked(summed_cols.reshape(nk, local_len, eb), 0, True).reshape(length, eb)
    skip_part = contract_rows(tok_halves[0], summed_cols[: length // 2]) + contract_rows(tok_halves[1], summed_cols[length // 2 :])
    skip_part, text_part, down_grad, result_part, up_grad = pin(
        (skip_part.astype(BF), text_part, down_grad, result_part, up_grad)
    )
    for bit in bits[1:]:
        half = result_part.shape[0] // 2
        result_part = result_part[:half] + flip(result_part[half:].astype(BF), "context", bit).astype(F32)
    result_low = (resid_two + (result_part + width_biases[4])).astype(BF)
    up_grad = spread(up_grad)
    skip_part = skip_part.reshape(2, nz, ny, -1, eb)
    keep = lax.dynamic_index_in_dim(skip_part, y, 2, keepdims=False)
    give = lax.dynamic_index_in_dim(skip_part, 1 - y, 2, keepdims=False)
    skip_total = (keep.astype(F32) + other(give).astype(F32)).astype(BF)
    skip_total, small_grad, triple_grad, result_low, summed_late, text_part = pin(
        (skip_total, small_grad, triple_grad, result_low, summed_low, text_part)
    )
    text_mine = lax.dynamic_slice_in_dim(text_part, y * text_cols, text_cols, 1)
    text_theirs = other(lax.dynamic_slice_in_dim(text_part, (1 - y) * text_cols, text_cols, 1))
    text_grad = by_batch(text_mine, text_theirs).astype(F32)
    skip_total = jnp.transpose(skip_total, (1, 0, 2, 3)).reshape(-1, eb)

    both_low = by_batch(summed_late, other(summed_late)).reshape(batch * local_len, nk, eb)
    skip_grad = lax.psum_scatter(skip_total, "shard", scatter_dimension=0, tiled=True)
    both_low, skip_grad = pin((ranked(both_low, 1, True), skip_grad))
    tok_grad, skip_rows_grad = [
        contract("tke,kde->td", both_low, w).reshape(batch, local_len, width)
        for w in (skip_all[:, :width], skip_all[:, width:])
    ]

    def place(parts, size, half, total):
        out = jnp.zeros(parts[0].shape[:-1] + (total,), F32)
        at = out.ndim - 1
        out = lax.dynamic_update_slice_in_dim(out, parts[0], k * size, at)
        return lax.dynamic_update_slice_in_dim(out, parts[1], half + k * size, at)

    def flattened(parts):
        flat = jnp.concatenate([p.reshape(-1) for p in parts])
        return jnp.pad(flat, (0, -flat.shape[0] % 1024)).reshape(-1, 128)

    def restored(flat, parts):
        flat, out, at = flat.reshape(-1), [], 0
        for p in parts:
            out.append(flat[at : at + p.size].reshape(p.shape))
            at += p.size
        return out

    def summed_over(flat, axis_name, bit, fill):
        got, fill = pin((flip(flat, axis_name, bit), fill))
        return flat + got, fill

    def col_sums(values, count=1):
        return jnp.sum(values.astype(F32), 0).reshape(count, -1)

    gains_grad = first_grads[2] + second_grads[1] + third_grads[1]
    biases_grad = first_grads[3] + second_grads[2] + third_grads[2]
    head_gain_grad = self_grads[1] + cross_grads[2]
    head_bias_grad = self_grads[2] + cross_grads[3]
    width_grad = jnp.stack(
        [
            jnp.sum(summed_low.astype(F32), 0),
            first_grads[1],
            jnp.sum(grad_one_low.astype(F32), 0),
            jnp.sum(grad_two_low.astype(F32), 0),
            jnp.sum(grad_out, 0),
        ]
    )
    column_parts = [
        jnp.concatenate([t, c], 0)
        for t, c in zip(
            [col_sums(t, 3) for t in triple_low],
            own_first([jnp.concatenate([col_sums(c, 1), col_sums(p, 2)], 0) for c, p in zip(cross_grad_low, pair_low)]),
        )
    ]
    column_grad = place(column_parts, cb, half_cols, width)
    hidden_grad_sum = place([col_sums(h)[0] for h in hidden_grad], hb, half_hidden, hidden_biases.shape[0])
    shift_slots = lax.dynamic_update_slice_in_dim(
        jnp.zeros((sequences, width), F32), first_grads[1][None], z * ny + y, 0
    )
    parts = (gains_grad, biases_grad, head_gain_grad, head_bias_grad, width_grad, column_grad, hidden_grad_sum, shift_slots)
    flat, skip_total = pin((flattened(parts), skip_total))
    for bit in bits:
        flat, (small_grad, triple_grad) = summed_over(flat, "context", bit, (small_grad, triple_grad))
    small_all, triple_all = gather_rows(small_grad[None]), gather_rows(triple_grad[None])
    triple_out = jnp.stack(placed_out(triple_all, cb, 0, 3), 1)
    small_out = (
        placed_out(small_all, cb, 4, 1, "prn,pnm->mr")[0],
        placed_out(small_all, cb, 0, 1)[0],
        jnp.stack(placed_out(small_all, cb, 1, 2), 1),
        placed_out(small_all, cb, 3, 1, "prn,pnm->mr")[0],
    )

    for i in range(ny.bit_length() - 1):
        flat, (tok_grad, result_low) = summed_over(flat, "tensor", 1 << i, (tok_grad, result_low))
    result_out = by_batch(result_low, other(result_low)).astype(F32)
    skip_gathered = gather_rows(skip_grad[None])
    for i in range(nz.bit_length() - 1):
        if i == 0:
            flat, (skip_rows_grad, skip_gathered) = summed_over(flat, "shard", 1, (skip_rows_grad, skip_gathered))
        else:
            flat, (triple_out, small_out) = summed_over(flat, "shard", 1 << i, (triple_out, small_out))
    vectors = restored(flat, parts)
    skip_grad_out = placed_out(skip_gathered, eb, 0, 1)[0].reshape(2, -1, width)
    shift_grad_out = lax.dot_general(
        silu_rows.astype(F32), vectors[7], (((0,), (0,)), ((), ())), precision=lax.Precision.HIGHEST
    )

    return (
        result_out,
        tok_grad,
        skip_rows_grad,
        text_grad,
        skip_grad_out,
        shift_grad_out,
        triple_out,
        *small_out,
        wide_out(up_grad),
        wide_out(down_grad).T,
    ) + tuple(vectors[:7])


def solution(mesh):
    placed = (
        P("shard", "context", None),
        P("shard", "context", None),
        P("shard", None, None),
        P("shard", "context", None),
        P("shard"),
        P("shard", "context", None),
        P(None, ("shard", "tensor"), None),
        P(("shard", "tensor"), None),
        P("shard", None, "tensor"),
        P("tensor", "shard"),
        P("shard", "tensor"),
        P("shard", None, "tensor"),
        P("tensor", "shard"),
        P("shard", "tensor"),
        P("tensor", "shard"),
    ) + (P(),) * 7
    return jax.shard_map(
        on_device,
        mesh=mesh,
        in_specs=placed,
        out_specs=(
            P("shard", "context", None),
            P("shard", "context", None),
            P("shard", "context", None),
            P("shard", None, ("context", "tensor")),
        )
        + placed[6:15]
        + (P(),) * 7,
        check_vma=False,
    )
```
